512 devices in a mesh: dp: 16 (over y, core), seq: 32 (over z, x).
Axes of the slice: x: 4, y: 8, z: 8, core: 2. Of those that a mesh axis runs over, the one named last changes fastest.
Arguments:
- query: bfloat16 [65536, 1536], P(('dp', 'seq')), may hold values from -100 to 100
- key: bfloat16 [65536, 1536], P(('dp', 'seq')), may hold values from -5 to 5
- value: bfloat16 [65536, 1536], P(('dp', 'seq')), may hold values from -6 to 6
- text: bfloat16 [4096, 512], P(('dp', 'seq')), may hold values from -6 to 6
- cond_weight: bfloat16 [512, 1536], P(('dp', 'seq')), may hold values from -0.25 to 0.25
- cotangent: bfloat16 [65536, 1536], P(('dp', 'seq')), may hold values from -6 to 6
- dest: int32 [65536], P(('dp', 'seq')), may hold values from 0 to 8191, as said below
- segment: int32 [131072], P(('dp', 'seq')), may hold values from -1 to 8191, as said below
- align: int32 [65536], P(('dp', 'seq')), may hold values from 0 to 255
Outputs:
- attended: bfloat16 [65536, 1536], P(('dp', 'seq'))
- query_grad: bfloat16 [65536, 1536], P(('dp', 'seq'))
- key_grad: bfloat16 [65536, 1536], P(('dp', 'seq'))
- value_grad: bfloat16 [65536, 1536], P(('dp', 'seq'))
- text_grad: float32 [4096, 512], P(('dp', 'seq'))
- weight_grad: float32 [512, 1536], P(('dp', 'seq'))
The draws below stay inside these ranges and needn't reach their ends.
Inputs may be any that keep to these rules, and one draw needn't show every extreme that they name: `dest`: within each batch the entries are distinct; every device sends exactly 8 frames to each of exactly 16 owners; an owner's used slots are 0 upwards without gaps, either none or 192 to 256 of them; some owner of every batch has all 256 slots used and some none. `segment`: -1 exactly on unused slots; an utterance's slots are consecutive and lie on one owner; ids are distinct across owners.
All inputs are finite; a program needn't handle non-finite values.
Results may differ from the reference program's by a relative error of at most 0.013.
Values may be sent and summed in bfloat16 or wider, within the bound.
No kernel may reach another device: no remote copies, remote signals or barrier semaphores. Data moves between devices by JAX's collectives and lax.ppermute only.
A program may use at most 64 MiB of HBM per device.

```python
import jax
import jax.numpy as jnp
from jax import lax

HEADS = 12
HEAD_DIM = 128
TEXT_DIM = 512
ROWS_DEV = 128
TEXT_DEV = 8
SLOTS = 256
BUCKET = 8
WIDTH = 1536
TOKENS = 65536
GROUP_TEXT = 256
TEXTS = 4096
N_DP = 16
N_SEQ = 32


def attention_pair(key):
    shape = (TOKENS, HEADS * HEAD_DIM)
    keys = jnp.clip(jax.random.normal(jax.random.fold_in(key, 11), shape, jnp.float32), -5.0, 5.0)
    others = jnp.clip(jax.random.normal(jax.random.fold_in(key, 12), shape, jnp.float32), -5.0, 5.0)
    queries = others
    return (queries, keys)


def draw_query(key, part):
    return attention_pair(key)[0].astype(jnp.bfloat16)


def draw_key(key, part):
    return attention_pair(key)[1].astype(jnp.bfloat16)


def one_batch(batch_key):
    peers = N_SEQ
    half = N_SEQ // 2
    quarter = N_SEQ // 4
    groups = N_SEQ // 8
    first, second, third = jax.random.split(batch_key, 3)
    order = jax.random.permutation(first, peers)
    pattern = jnp.array([3, 3, 3, 3, 3, 0, 0, 0], jnp.int32) * quarter
    extra_one = jax.random.randint(second, (groups,), 0, quarter + 1).at[0].set(quarter)
    layout = jnp.tile(pattern[None, :], (groups, 1))
    layout = layout.at[:, 0].add(extra_one).at[:, 1].add(quarter - extra_one)
    degree = jnp.zeros((peers,), jnp.int32).at[order].set(layout.reshape(-1))
    ends = jnp.cumsum(degree)
    starts = ends - degree
    entry = jnp.arange(peers * half)
    owner_of = jnp.sum((entry[:, None] >= ends[None, :]).astype(jnp.int32), axis=1)
    rank_of = entry - starts[owner_of]
    owners = owner_of.reshape(half, peers).T
    ranks = rank_of.reshape(half, peers).T
    inside = jnp.arange(BUCKET)
    targets = (owners[:, :, None] * SLOTS + ranks[:, :, None] * BUCKET + inside[None, None, :]).reshape(peers, ROWS_DEV)
    shuffles = jax.vmap(lambda sub: jax.random.permutation(sub, ROWS_DEV))(jax.random.split(third, peers))
    targets = jnp.take_along_axis(targets, shuffles, axis=1)
    slot = jnp.arange(SLOTS)
    used = slot[None, :] < (degree * BUCKET)[:, None]
    owner_used = (degree > 0).astype(jnp.int32)
    counter = jnp.cumsum(owner_used) - 1
    owner_label = peers * SLOTS - 1 - counter * SLOTS
    labels = jnp.where(used, owner_label[:, None], -1).reshape(-1)
    return (targets.reshape(-1), labels)


def packing(key):
    batch_keys = jax.random.split(jax.random.fold_in(key, 21), N_DP)
    targets, labels = jax.vmap(one_batch)(batch_keys)
    return (targets.reshape(-1).astype(jnp.int32), labels.reshape(-1).astype(jnp.int32))


def draw_dest(key, part):
    return packing(key)[0]


def draw_segment(key, part):
    return packing(key)[1]


def touch_ends(result, rng, smallest, high):
    spot = [jax.random.randint(jax.random.fold_in(rng, axis), (), 0, length) for axis, length in enumerate(result.shape)]
    widest = result.shape.index(max(result.shape))
    neighbour = spot[:widest] + [(spot[widest] + 1) % result.shape[widest]] + spot[widest + 1:]
    return result.at[tuple(spot)].set(smallest).at[tuple(neighbour)].set(high)


def level_of(key, extent, pieces, smallest, largest):
    loudness = 1.0
    for dim, parts in pieces:
        steps = jax.random.uniform(jax.random.fold_in(jax.random.fold_in(key, 6), dim), (parts,), jnp.float32, smallest / len(pieces), largest / len(pieces))
        loudness = loudness * jnp.repeat(jnp.exp(steps), extent[dim] // parts).reshape((-1,) + (1,) * (len(extent) - 1 - dim))
    return loudness


def normal_values(own_key, shape, scale, reach, shards=(), kind=jnp.bfloat16):
    gain = level_of(own_key, shape, shards, -0.22, 0.18) if shards else 1.0
    drawn = jax.random.normal(own_key, shape, jnp.float32) * scale * gain
    return jnp.minimum(jnp.maximum(drawn, -reach), reach).astype(kind)


def setup_inputs(seed: int = 0) -> dict:
    arg_keys = jax.random.split(jax.random.key(seed), 10)
    query = draw_query(jax.random.fold_in(arg_keys[9], 71), 0)
    key = draw_key(jax.random.fold_in(arg_keys[9], 71), 0)
    value = normal_values(arg_keys[2], (TOKENS, WIDTH), 1.0, 6.0, ((0, 512),))
    text = normal_values(arg_keys[3], (TEXTS, TEXT_DIM), 1.0, 6.0, ((0, 512),))
    cond_weight = normal_values(arg_keys[4], (TEXT_DIM, WIDTH), TEXT_DIM ** -0.5, 0.25, ((0, 512),))
    cotangent = normal_values(arg_keys[5], (TOKENS, WIDTH), 1.0, 6.0, ((0, 512),))
    dest = draw_dest(jax.random.fold_in(arg_keys[9], 71), 0)
    segment = draw_segment(jax.random.fold_in(arg_keys[9], 71), 0)
    align = touch_ends(jax.random.randint(arg_keys[8], (TOKENS,), 0, GROUP_TEXT), jax.random.fold_in(arg_keys[8], 1), 0, GROUP_TEXT - 1).astype(jnp.int32)
    return dict(query=query, key=key, value=value, text=text, cond_weight=cond_weight, cotangent=cotangent, dest=dest, segment=segment, align=align)


def attend(queries, keys, values, cotangents, labels):
    slots = queries.shape[0]
    width = queries.shape[1]
    size = width // HEADS
    scale = size ** -0.5
    qheads = queries.astype(jnp.float32).reshape(slots, HEADS, size)
    kheads = keys.astype(jnp.float32).reshape(slots, HEADS, size)
    vheads = values.astype(jnp.float32).reshape(slots, HEADS, size)
    gheads = cotangents.astype(jnp.float32).reshape(slots, HEADS, size)
    index = jnp.arange(slots)
    allowed = ((labels[:, None] == labels[None, :]) & (labels[:, None] >= 0)) | (index[:, None] == index[None, :])
    scores = jnp.einsum("qhd,khd->hqk", qheads, kheads) * scale
    scores = jnp.where(allowed[None], scores, -1e30)
    top = jnp.max(scores, axis=2, keepdims=True)
    expos = jnp.exp(scores - top)
    probs = expos / jnp.sum(expos, axis=2, keepdims=True)
    weights = probs.astype(jnp.bfloat16).astype(jnp.float32)
    outputs = jnp.einsum("hqk,khd->qhd", weights, vheads).astype(jnp.bfloat16)
    value_part = jnp.einsum("hqk,qhd->khd", weights, gheads).astype(jnp.bfloat16)
    prob_grad = jnp.einsum("qhd,khd->hqk", gheads, vheads)
    centre = jnp.sum(probs * prob_grad, axis=2, keepdims=True)
    score_grad = (probs * (prob_grad - centre)).astype(jnp.bfloat16).astype(jnp.float32)
    query_part = (jnp.einsum("hqk,khd->qhd", score_grad, kheads) * scale).astype(jnp.bfloat16)
    key_part = (jnp.einsum("hqk,qhd->khd", score_grad, qheads) * scale).astype(jnp.bfloat16)
    return (outputs.reshape(slots, width), query_part.reshape(slots, width),
            key_part.reshape(slots, width), value_part.reshape(slots, width))


def reference(query, key, value, text, cond_weight, cotangent, dest, segment, align):
    group = N_SEQ * ROWS_DEV
    width = HEADS * HEAD_DIM

    def one_group(items):
        queries, keys, values, text_rows, cotangents, targets, labels, picks = items
        condition = jnp.take(text_rows, picks, axis=0)
        extra = jnp.dot(condition, cond_weight, preferred_element_type=jnp.float32)
        valued = (values.astype(jnp.float32) + extra).astype(jnp.bfloat16)

        def settle(rows_in):
            placed = jnp.zeros((N_SEQ * SLOTS, width), rows_in.dtype).at[targets].set(rows_in)
            return placed.reshape(N_SEQ, SLOTS, width)

        owners = (settle(queries), settle(keys), settle(valued), settle(cotangents), labels.reshape(N_SEQ, SLOTS))
        results = lax.map(lambda block: attend(*block), owners)
        flat = [res.reshape(N_SEQ * SLOTS, width)[targets] for res in results]
        value_grad = flat[3]
        cond_grad = jnp.dot(value_grad, cond_weight.T, preferred_element_type=jnp.float32)
        text_part = jnp.zeros((N_SEQ * TEXT_DEV, TEXT_DIM), jnp.float32).at[picks].add(cond_grad)
        weight_part = jnp.dot(condition.T, value_grad, preferred_element_type=jnp.float32)
        return flat[0], flat[1], flat[2], value_grad, text_part, weight_part

    items = (query.reshape(N_DP, group, width), key.reshape(N_DP, group, width),
             value.reshape(N_DP, group, width), text.reshape(N_DP, N_SEQ * TEXT_DEV, TEXT_DIM),
             cotangent.reshape(N_DP, group, width), dest.reshape(N_DP, group),
             segment.reshape(N_DP, N_SEQ * SLOTS), align.reshape(N_DP, group))
    outs = lax.map(one_group, items)
    attended = outs[0].reshape(N_DP * group, width)
    query_grad = outs[1].reshape(N_DP * group, width)
    key_grad = outs[2].reshape(N_DP * group, width)
    value_grad = outs[3].reshape(N_DP * group, width)
    text_grad = outs[4].reshape(N_DP * N_SEQ * TEXT_DEV, TEXT_DIM)
    weight_grad = jnp.sum(outs[5], axis=0)
    return attended, query_grad, key_grad, value_grad, text_grad, weight_grad
```

```python
import functools

import jax
import jax.numpy as jnp
from jax import lax
from jax.experimental import pallas as pl
from jax.experimental.pallas import tpu as pltpu
from jax.sharding import PartitionSpec as P

F32 = jnp.float32
BF16 = jnp.bfloat16

NZ, NX = 8, 4
PEERS = NZ * NX
ROWS = 128
SLOTS = 256
BUCKET = 8
OWN = 3
HPD = 3
COMPACT = NZ * OWN
LANES = 128
COLS = HPD * LANES
TEXT = 512
GTEXT = 256
BLOCK = 2 * HPD * 2 * BUCKET
TG_ROWS = 32
OUT_ROWS = OWN * BLOCK + TG_ROWS


def iota(shape, dim):
    return lax.broadcasted_iota(jnp.int32, shape, dim)


def dot(a, b):
    return jnp.dot(a, b, preferred_element_type=F32)


def dot_nt(a, b):
    return lax.dot_general(a, b, (((1,), (1,)), ((), ())), preferred_element_type=F32)


def dot_tn(a, b):
    return lax.dot_general(a, b, (((0,), (0,)), ((), ())), preferred_element_type=F32)


def upper(n):
    return (iota((n, n), 0) <= iota((n, n), 1)).astype(BF16)


def spread8(x):
    n = x.shape[0]
    return jnp.broadcast_to(x[:, None, :], (n, BUCKET, LANES)).reshape(n * BUCKET, LANES)


def bucket_select(match):
    n = match.shape[0]
    count = dot(match.astype(BF16), upper(ROWS))
    rank = ((iota((n * BUCKET, LANES), 0) & (BUCKET - 1)) + 1).astype(F32)
    hit = (spread8(count) == rank) & (spread8(match) > 0.5)
    return jnp.where(hit, 1.0, 0.0)


def compact_owners(seg_first):
    flag = jnp.where(jnp.broadcast_to(seg_first[:, 0:1], (PEERS, LANES)) >= 0.0, 1.0, 0.0)
    lower = (iota((PEERS, PEERS), 0) >= iota((PEERS, PEERS), 1)).astype(BF16)
    count = dot(lower, flag.astype(BF16))
    lane = (iota((PEERS, LANES), 1) + 1).astype(F32)
    hit = jnp.where((count == lane) & (flag > 0.5), 1.0, 0.0)
    ids = iota((PEERS, LANES), 0).astype(F32) + 1.0
    row = jnp.sum(hit * ids, axis=0, keepdims=True) - 1.0
    diag = iota((COMPACT, LANES), 0) == iota((COMPACT, LANES), 1)
    col = jnp.sum(jnp.where(diag, jnp.broadcast_to(row, (COMPACT, LANES)), 0.0), axis=1, keepdims=True)
    return jnp.broadcast_to(col, (COMPACT, LANES))


def prep_kernel(dest_ref, align_ref, seg_ref, w_ref, out_ref):
    sub = iota((8, LANES), 0)

    def row(v):
        return jnp.broadcast_to(v.astype(F32), (8, LANES))

    base = jnp.where(sub == 0, row(dest_ref[...]), 0.0)
    base = jnp.where(sub == 1, row(align_ref[...]), base)
    seg = seg_ref[...]
    base = jnp.where(sub == 2, row(seg[:, :LANES]), base)
    base = jnp.where(sub == 3, row(seg[:, LANES:]), base)
    w = w_ref[...].astype(F32)
    for x in range(NX):
        msg = base
        for h in range(HPD):
            start = (x * HPD + h) * LANES
            msg = jnp.where(sub == 4 + h, row(w[:, start : start + LANES]), msg)
        for z in range(NZ):
            out_ref[z, x] = msg


def prep(dest, align, seg, w):
    return pl.pallas_call(
        prep_kernel,
        out_shape=jax.ShapeDtypeStruct((NZ, NX, 8, LANES), F32),
        name="prep",
    )(dest, align, seg, w)


def owner_match(msg_ref, dest_ref):
    owners = compact_owners(msg_ref[pl.ds(2, PEERS, stride=8), :])
    mine = jnp.broadcast_to(dest_ref[...] >> 8, (COMPACT, LANES)).astype(F32)
    return owners, jnp.where(mine == owners, 1.0, 0.0)


def pack_kernel(msg_ref, dest_ref, q_ref, k_ref, v_ref, g_ref, out_ref, own_ref, sel_ref):
    @pl.when(pl.program_id(0) == 0)
    def _():
        owners, match = owner_match(msg_ref, dest_ref)
        own_ref[...] = owners
        sel_ref[...] = bucket_select(match).astype(BF16)

    sel = sel_ref[...]
    for pair, (a_ref, b_ref) in enumerate(((q_ref, k_ref), (v_ref, g_ref))):
        a = dot(sel, a_ref[...]).reshape(COMPACT, BUCKET, COLS)
        b = dot(sel, b_ref[...]).reshape(COMPACT, BUCKET, COLS)
        both = jnp.concatenate([a, b], axis=1).astype(BF16).reshape(NZ, OWN, 2 * BUCKET, COLS)
        for i in range(OWN):
            for h in range(HPD):
                off = i * BLOCK + (pair * HPD + h) * 2 * BUCKET
                out_ref[:, 0, off : off + 2 * BUCKET, :] = both[:, i, :, h * LANES : (h + 1) * LANES]


def pack(msg, dest, q, k, v, g):
    full = lambda shape: pl.BlockSpec(shape, lambda x: (0,) * len(shape))
    cols = pl.BlockSpec((ROWS, COLS), lambda x: (0, x))
    return pl.pallas_call(
        pack_kernel,
        grid=(NX,),
        in_specs=[full((PEERS * 8, LANES)), full((1, LANES)), cols, cols, cols, cols],
        out_specs=[
            pl.BlockSpec((NZ, 1, OWN * BLOCK, LANES), lambda x: (0, x, 0, 0)),
            full((COMPACT, LANES)),
        ],
        out_shape=[
            jax.ShapeDtypeStruct((NZ, NX, OWN * BLOCK, LANES), BF16),
            jax.ShapeDtypeStruct((COMPACT, LANES), F32),
        ],
        scratch_shapes=[pltpu.VMEM((COMPACT * BUCKET, LANES), BF16)],
        name="pack",
    )(msg, dest, q, k, v, g)


def attend_kernel(z_ref, msg_ref, own_ref, in_ref, text_ref, w_ref, out_ref, wg_ref, acc_ref):
    i = pl.program_id(0)
    n = SLOTS

    owner = jnp.broadcast_to(own_ref[pl.ds(z_ref[0] * OWN + i, 1), :], (PEERS, LANES))
    dest = msg_ref[pl.ds(0, PEERS, stride=8), :].astype(jnp.int32)
    match = jnp.where((dest >> 8).astype(F32) == owner, 1.0, 0.0)
    sel = bucket_select(match)
    valid = jnp.sum(sel, axis=1, keepdims=True)
    slot = jnp.sum(sel * spread8((dest & (SLOTS - 1)).astype(F32)), axis=1, keepdims=True)
    slot = jnp.where(valid > 0.5, slot, -1.0)
    align = jnp.sum(sel * spread8(msg_ref[pl.ds(1, PEERS, stride=8), :]), axis=1, keepdims=True)
    align = jnp.where(valid > 0.5, align, -1.0)

    mine = iota((PEERS, LANES), 0).astype(F32) == owner
    seg_lo = jnp.sum(jnp.where(mine, msg_ref[pl.ds(2, PEERS, stride=8), :], 0.0), axis=0, keepdims=True)
    seg_hi = jnp.sum(jnp.where(mine, msg_ref[pl.ds(3, PEERS, stride=8), :], 0.0), axis=0, keepdims=True)
    seg = jnp.concatenate([seg_lo, seg_hi], axis=1)
    lane = iota((n, n), 1)
    lanef = lane.astype(F32)
    diag = iota((n, n), 0) == lane
    label = jnp.sum(jnp.where(lanef == slot, jnp.broadcast_to(seg, (n, n)), 0.0), axis=1, keepdims=True)
    label = jnp.where(valid > 0.5, label, -1.0)
    label_b = jnp.broadcast_to(label, (n, n))
    label_row = jnp.sum(jnp.where(diag, label_b, 0.0), axis=0, keepdims=True)
    allowed = ((label_b == jnp.broadcast_to(label_row, (n, n))) & (label_b >= 0.0)) | diag
    bias = jnp.where(allowed, 0.0, -1e30)

    pick = jnp.where(lanef == align, 1.0, 0.0).astype(BF16)
    cond = dot(pick, text_ref[...]).astype(BF16)
    extra = dot(cond, w_ref[...])

    scale = LANES ** (-0.5)

    def pair_of(pair, h):
        off = (pair * HPD + h) * 2 * BUCKET
        both = in_ref[:, off : off + 2 * BUCKET, :].astype(F32).reshape(PEERS, 2, BUCKET, LANES)
        return both[:, 0].reshape(n, LANES), both[:, 1].reshape(n, LANES)

    def put(pair, h, a, b):
        off = (pair * HPD + h) * 2 * BUCKET
        both = jnp.concatenate(
            [a.reshape(PEERS, BUCKET, LANES), b.reshape(PEERS, BUCKET, LANES)], axis=1
        ).astype(BF16)
        out_ref[:, pl.ds(pl.multiple_of(i * BLOCK + off, 16), 2 * BUCKET), :] = both

    value_grads = []
    for h in range(HPD):
        q, k = pair_of(0, h)
        v, g = pair_of(1, h)
        q, k, g = q.astype(BF16), k.astype(BF16), g.astype(BF16)
        v = (v + extra[:, h * LANES : (h + 1) * LANES]).astype(BF16)
        s = dot_nt(q, k) * scale + bias
        e = jnp.exp(s - jnp.max(s, axis=1, keepdims=True))
        p = e * (1.0 / jnp.sum(e, axis=1, keepdims=True))
        w = p.astype(BF16)
        out = dot(w, v)
        value_grad = dot_tn(w, g)
        pg = dot_nt(g, v)
        centre = jnp.sum(p * pg, axis=1, keepdims=True)
        sg = (p * (pg - centre)).astype(BF16)
        query_grad = dot(sg, k) * scale
        key_grad = dot_tn(sg, q) * scale
        put(0, h, out, query_grad)
        put(1, h, key_grad, value_grad)
        value_grads.append(value_grad.astype(BF16))

    part = dot_tn(pick, jnp.concatenate(value_grads, axis=1))

    @pl.when(i == 0)
    def _():
        acc_ref[...] = part

    @pl.when(i > 0)
    def _():
        acc_ref[...] += part

    @pl.when(i == OWN - 1)
    def _():
        acc = acc_ref[...]
        high = acc.astype(BF16)
        low = (acc - high.astype(F32)).astype(BF16)
        weight = w_ref[...]
        tg = dot_nt(high, weight) + dot_nt(low, weight)
        tg = tg.reshape(PEERS, BUCKET, TEXT)
        for c in range(2):
            both = jnp.concatenate(
                [tg[:, :, 2 * c * LANES : (2 * c + 1) * LANES], tg[:, :, (2 * c + 1) * LANES : (2 * c + 2) * LANES]],
                axis=1,
            ).astype(BF16)
            off = OWN * BLOCK + c * 2 * BUCKET
            out_ref[:, off : off + 2 * BUCKET, :] = both
        text = text_ref[...]
        wg_ref[...] = dot_tn(text, high) + dot_tn(text, low)


def attend(zi, msg, own, got, text, w):
    full = lambda shape: pl.BlockSpec(shape, lambda i, z: (0,) * len(shape))
    return pl.pallas_call(
        attend_kernel,
        grid_spec=pltpu.PrefetchScalarGridSpec(
            num_scalar_prefetch=1,
            grid=(OWN,),
            in_specs=[
                full((PEERS * 8, LANES)),
                full((COMPACT, LANES)),
                pl.BlockSpec((PEERS, BLOCK, LANES), lambda i, z: (0, i, 0)),
                full((GTEXT, TEXT)),
                full((TEXT, COLS)),
            ],
            out_specs=[full((PEERS, OUT_ROWS, LANES)), full((TEXT, COLS))],
            scratch_shapes=[pltpu.VMEM((GTEXT, COLS), F32)],
        ),
        out_shape=[
            jax.ShapeDtypeStruct((PEERS, OUT_ROWS, LANES), BF16),
            jax.ShapeDtypeStruct((TEXT, COLS), F32),
        ],
        name="attend",
    )(zi, msg, own, got, text, w)


def unpack_kernel(msg_ref, dest_ref, in_ref, o_ref, q_ref, k_ref, v_ref, tg_ref, sel_ref):
    x = pl.program_id(0)

    @pl.when(x == 0)
    def _():
        _, match = owner_match(msg_ref, dest_ref)
        sel_ref[...] = jnp.transpose(bucket_select(match)).astype(BF16)

    sel = sel_ref[...]
    for pair, (a_ref, b_ref) in enumerate(((o_ref, q_ref), (k_ref, v_ref))):
        for h in range(HPD):
            parts = []
            for i in range(OWN):
                off = i * BLOCK + (pair * HPD + h) * 2 * BUCKET
                parts.append(
                    in_ref[:, 0, off : off + 2 * BUCKET, :].astype(F32).reshape(NZ, 1, 2, BUCKET, LANES)
                )
            both = jnp.concatenate(parts, axis=1)
            a = both[:, :, 0].reshape(COMPACT * BUCKET, LANES).astype(BF16)
            b = both[:, :, 1].reshape(COMPACT * BUCKET, LANES).astype(BF16)
            span = slice(h * LANES, (h + 1) * LANES)
            a_ref[:, span] = dot(sel, a).astype(BF16)
            b_ref[:, span] = dot(sel, b).astype(BF16)

    for c in range(2):
        off = OWN * BLOCK + c * 2 * BUCKET
        total = jnp.sum(in_ref[:, 0, off : off + 2 * BUCKET, :].astype(F32), axis=0)
        for half in range(2):
            span = slice((2 * c + half) * LANES, (2 * c + half + 1) * LANES)
            piece = total[half * BUCKET : (half + 1) * BUCKET]

            @pl.when(x == 0)
            def _():
                tg_ref[:, span] = piece

            @pl.when(x > 0)
            def _():
                tg_ref[:, span] += piece


def unpack(msg, dest, got):
    full = lambda shape: pl.BlockSpec(shape, lambda x: (0,) * len(shape))
    cols = pl.BlockSpec((ROWS, COLS), lambda x: (0, x))
    rows = jax.ShapeDtypeStruct((ROWS, NX * COLS), BF16)
    return pl.pallas_call(
        unpack_kernel,
        grid=(NX,),
        in_specs=[
            full((PEERS * 8, LANES)),
            full((1, LANES)),
            pl.BlockSpec((NZ, 1, OUT_ROWS, LANES), lambda x: (0, x, 0, 0)),
        ],
        out_specs=[cols, cols, cols, cols, full((BUCKET, TEXT))],
        out_shape=[rows, rows, rows, rows, jax.ShapeDtypeStruct((BUCKET, TEXT), F32)],
        scratch_shapes=[pltpu.VMEM((ROWS, COMPACT * BUCKET), BF16)],
        name="unpack",
    )(msg, dest, got)


def exchange(x):
    return lax.all_to_all(x, "seq", split_axis=0, concat_axis=0, tiled=True)


def swap(x, axis, bit):
    size = lax.axis_size(axis)
    return lax.ppermute(x, axis, [(j, j ^ bit) for j in range(size)])


def gather_bits(x, axis, bits):
    index = lax.axis_index(axis)
    for depth, bit in enumerate(bits):
        other = swap(x, axis, bit)
        up = (index & bit) != 0
        first = jnp.where(up, other, x)
        second = jnp.where(up, x, other)
        x = jnp.stack([first, second], axis=depth)
    return x


def halve(x, axis, bit, dim):
    up = (lax.axis_index(axis) & bit) != 0
    zero, one = lax.index_in_dim(x, 0, dim, False), lax.index_in_dim(x, 1, dim, False)
    return jnp.where(up, one, zero) + swap(jnp.where(up, zero, one), axis, bit)


def local(query, key, value, text, cond_weight, cotangent, dest, segment, align):
    seq = lax.axis_index("seq")
    zi = (seq // NX).astype(jnp.int32).reshape(1)
    xi = seq % NX
    dest_row = dest.reshape(1, ROWS)
    first = prep(dest_row, align.reshape(1, ROWS), segment.reshape(1, SLOTS), cond_weight)
    msg3 = exchange(first.reshape(PEERS, 8, LANES))
    msg = msg3.reshape(PEERS * 8, LANES)
    packed, own = pack(msg, dest_row, query, key, value, cotangent)
    got = exchange(packed.reshape(PEERS, OWN * BLOCK, LANES))
    my_w = msg3[:, 4 : 4 + HPD, :].astype(BF16).reshape(PEERS, COLS)
    full_w = gather_bits(my_w, "dp", (8, 4, 2, 1)).reshape(TEXT, COLS)
    full_text = gather_bits(text, "seq", (16, 8, 4, 2, 1)).reshape(GTEXT, TEXT)
    back, wg = attend(zi, msg, own, got, full_text, full_w)
    returned = exchange(back)
    wg = wg.reshape(2, 2, 2, 2, PEERS, COLS)
    for bit, dim in ((1, 3), (2, 2), (4, 1), (8, 0)):
        wg = halve(wg, "dp", bit, dim)
    wg = wg.reshape(2, 2, 2, NX, COLS)
    for bit, dim in ((4, 2), (8, 1), (16, 0)):
        wg = halve(wg, "seq", bit, dim)
    pieces = [lax.dynamic_index_in_dim(wg, xi, 0, True)]
    for flip in (1, 2, 3):
        row = lax.dynamic_index_in_dim(wg, xi ^ flip, 0, True)
        pieces.append(swap(row, "seq", flip))
    out_cols = []
    for c in range(NX):
        flip = xi ^ c
        col = pieces[0]
        for m in (1, 2, 3):
            col = jnp.where(flip == m, pieces[m], col)
        out_cols.append(col)
    weight_grad = jnp.concatenate(out_cols, axis=1)
    attended, query_grad, key_grad, value_grad, text_grad = unpack(
        msg, dest_row, returned.reshape(NZ, NX, OUT_ROWS, LANES)
    )
    return attended, query_grad, key_grad, value_grad, text_grad, weight_grad


def solution(mesh):
    rows = P(("dp", "seq"), None)
    flat = P(("dp", "seq"))
    return jax.shard_map(
        local,
        mesh=mesh,
        in_specs=(rows, rows, rows, rows, rows, rows, flat, flat, flat),
        out_specs=(rows,) * 6,
        check_vma=False,
    )
```

```python
import jax
import jax.numpy as jnp
from jax import lax
from jax.experimental import pallas as pl
from jax.experimental.pallas import tpu as pltpu
from jax.sharding import PartitionSpec as P

F32 = jnp.float32
BF16 = jnp.bfloat16

NZ, NX = 8, 4
PEERS = NZ * NX
ROWS = 128
SLOTS = 256
BUCKET = 8
OWN = 3
HPD = 3
COMPACT = NZ * OWN
LANES = 128
COLS = HPD * LANES
TEXT = 512
GTEXT = 256
BLOCK = 2 * HPD * 2 * BUCKET
TEXT_ROWS = 32
MSG_ROWS = OWN * BLOCK + TEXT_ROWS


def iota(shape, dim):
    return lax.broadcasted_iota(jnp.int32, shape, dim)


def dot(a, b):
    return jnp.dot(a, b, preferred_element_type=F32)


def dot_nt(a, b):
    return lax.dot_general(a, b, (((1,), (1,)), ((), ())), preferred_element_type=F32)


def dot_tn(a, b):
    return lax.dot_general(a, b, (((0,), (0,)), ((), ())), preferred_element_type=F32)


def upper(n):
    return (iota((n, n), 0) <= iota((n, n), 1)).astype(BF16)


def spread8(x):
    n = x.shape[0]
    return jnp.broadcast_to(x[:, None, :], (n, BUCKET, LANES)).reshape(n * BUCKET, LANES)


def bucket_select(match):
    n = match.shape[0]
    count = dot(match.astype(BF16), upper(ROWS))
    rank = ((iota((n * BUCKET, LANES), 0) & (BUCKET - 1)) + 1).astype(F32)
    hit = (spread8(count) == rank) & (spread8(match) > 0.5)
    return jnp.where(hit, 1.0, 0.0)


def compact_owners(seg_first):
    flag = jnp.where(jnp.broadcast_to(seg_first[:, 0:1], (PEERS, LANES)) >= 0.0, 1.0, 0.0)
    lower = (iota((PEERS, PEERS), 0) >= iota((PEERS, PEERS), 1)).astype(BF16)
    count = dot(lower, flag.astype(BF16))
    lane = (iota((PEERS, LANES), 1) + 1).astype(F32)
    hit = jnp.where((count == lane) & (flag > 0.5), 1.0, 0.0)
    ids = iota((PEERS, LANES), 0).astype(F32) + 1.0
    row = jnp.sum(hit * ids, axis=0, keepdims=True) - 1.0
    diag = iota((COMPACT, LANES), 0) == iota((COMPACT, LANES), 1)
    col = jnp.sum(jnp.where(diag, jnp.broadcast_to(row, (COMPACT, LANES)), 0.0), axis=1, keepdims=True)
    return jnp.broadcast_to(col, (COMPACT, LANES))


def prep_kernel(dest_ref, align_ref, seg_ref, w_ref, out_ref):
    sub = iota((8, LANES), 0)

    def row(v):
        return jnp.broadcast_to(v.astype(F32), (8, LANES))

    base = jnp.where(sub == 0, row(dest_ref[...]), 0.0)
    base = jnp.where(sub == 1, row(align_ref[...]), base)
    seg = seg_ref[...]
    base = jnp.where(sub == 2, row(seg[:, :LANES]), base)
    base = jnp.where(sub == 3, row(seg[:, LANES:]), base)
    w = w_ref[...].astype(F32)
    for x in range(NX):
        msg = base
        for h in range(HPD):
            start = (x * HPD + h) * LANES
            msg = jnp.where(sub == 4 + h, row(w[:, start : start + LANES]), msg)
        for z in range(NZ):
            out_ref[z, x] = msg


def prep(dest, align, seg, w):
    return pl.pallas_call(
        prep_kernel,
        out_shape=jax.ShapeDtypeStruct((NZ, NX, 8, LANES), F32),
        name="prep",
    )(dest, align, seg, w)


def owner_match(msg_ref, dest_ref):
    owners = compact_owners(msg_ref[pl.ds(2, PEERS, stride=8), :])
    mine = jnp.broadcast_to(dest_ref[...] >> 8, (COMPACT, LANES)).astype(F32)
    return owners, jnp.where(mine == owners, 1.0, 0.0)


def pack_kernel(msg_ref, dest_ref, text_ref, q_ref, k_ref, v_ref, g_ref, out_ref, own_ref, sel_ref):
    @pl.when(pl.program_id(0) == 0)
    def _():
        owners, match = owner_match(msg_ref, dest_ref)
        own_ref[...] = owners
        sel_ref[...] = bucket_select(match).astype(BF16)

    sel = sel_ref[...]
    for pair, (a_ref, b_ref) in enumerate(((q_ref, k_ref), (v_ref, g_ref))):
        a = dot(sel, a_ref[...]).reshape(COMPACT, BUCKET, COLS)
        b = dot(sel, b_ref[...]).reshape(COMPACT, BUCKET, COLS)
        both = jnp.concatenate([a, b], axis=1).astype(BF16).reshape(NZ, OWN, 2 * BUCKET, COLS)
        for i in range(OWN):
            for h in range(HPD):
                off = i * BLOCK + (pair * HPD + h) * 2 * BUCKET
                out_ref[:, 0, off : off + 2 * BUCKET, :] = both[:, i, :, h * LANES : (h + 1) * LANES]
    text = text_ref[...].astype(F32)
    for c in range(2):
        tile = jnp.concatenate(
            [text[:, 2 * c * LANES : (2 * c + 1) * LANES], text[:, (2 * c + 1) * LANES : (2 * c + 2) * LANES]], axis=0
        ).astype(BF16)
        off = OWN * BLOCK + c * 2 * BUCKET
        for z in range(NZ):
            out_ref[z, 0, off : off + 2 * BUCKET, :] = tile


def pack(msg, dest, text, q, k, v, g):
    full = lambda shape: pl.BlockSpec(shape, lambda x: (0,) * len(shape))
    cols = pl.BlockSpec((ROWS, COLS), lambda x: (0, x))
    return pl.pallas_call(
        pack_kernel,
        grid=(NX,),
        in_specs=[full((PEERS * 8, LANES)), full((1, LANES)), full((BUCKET, TEXT)), cols, cols, cols, cols],
        out_specs=[
            pl.BlockSpec((NZ, 1, MSG_ROWS, LANES), lambda x: (0, x, 0, 0)),
            full((COMPACT, LANES)),
        ],
        out_shape=[
            jax.ShapeDtypeStruct((NZ, NX, MSG_ROWS, LANES), BF16),
            jax.ShapeDtypeStruct((COMPACT, LANES), F32),
        ],
        scratch_shapes=[pltpu.VMEM((COMPACT * BUCKET, LANES), BF16)],
        name="pack",
    )(msg, dest, text, q, k, v, g)


def attend_kernel(z_ref, msg_ref, own_ref, in_ref, tail_ref, w_ref, out_ref, wg_ref, acc_ref, text_ref):
    i = pl.program_id(0)
    n = SLOTS

    owner = jnp.broadcast_to(own_ref[pl.ds(z_ref[0] * OWN + i, 1), :], (PEERS, LANES))
    dest = msg_ref[pl.ds(0, PEERS, stride=8), :].astype(jnp.int32)
    match = jnp.where((dest >> 8).astype(F32) == owner, 1.0, 0.0)
    sel = bucket_select(match)
    valid = jnp.sum(sel, axis=1, keepdims=True)
    slot = jnp.sum(sel * spread8((dest & (SLOTS - 1)).astype(F32)), axis=1, keepdims=True)
    slot = jnp.where(valid > 0.5, slot, -1.0)
    align = jnp.sum(sel * spread8(msg_ref[pl.ds(1, PEERS, stride=8), :]), axis=1, keepdims=True)
    align = jnp.where(valid > 0.5, align, -1.0)

    mine = iota((PEERS, LANES), 0).astype(F32) == owner
    seg_lo = jnp.sum(jnp.where(mine, msg_ref[pl.ds(2, PEERS, stride=8), :], 0.0), axis=0, keepdims=True)
    seg_hi = jnp.sum(jnp.where(mine, msg_ref[pl.ds(3, PEERS, stride=8), :], 0.0), axis=0, keepdims=True)
    seg = jnp.concatenate([seg_lo, seg_hi], axis=1)
    lane = iota((n, n), 1)
    lanef = lane.astype(F32)
    diag = iota((n, n), 0) == lane
    label = jnp.sum(jnp.where(lanef == slot, jnp.broadcast_to(seg, (n, n)), 0.0), axis=1, keepdims=True)
    label = jnp.where(valid > 0.5, label, -1.0)
    label_b = jnp.broadcast_to(label, (n, n))
    label_row = jnp.sum(jnp.where(diag, label_b, 0.0), axis=0, keepdims=True)
    allowed = ((label_b == jnp.broadcast_to(label_row, (n, n))) & (label_b >= 0.0)) | diag
    bias = jnp.where(allowed, 0.0, -1e30)

    @pl.when(i == 0)
    def _():
        for c in range(2):
            tiles = tail_ref[:, c * 2 * BUCKET : (c + 1) * 2 * BUCKET, :].astype(F32)
            tiles = tiles.reshape(PEERS, 2, BUCKET, LANES)
            for half in range(2):
                span = slice((2 * c + half) * LANES, (2 * c + half + 1) * LANES)
                text_ref[:, span] = tiles[:, half].reshape(GTEXT, LANES).astype(BF16)

    pick = jnp.where(lanef == align, 1.0, 0.0).astype(BF16)
    cond = dot(pick, text_ref[...]).astype(BF16)
    extra = dot(cond, w_ref[...])

    scale = LANES ** (-0.5)

    def pair_of(pair, h):
        off = (pair * HPD + h) * 2 * BUCKET
        both = in_ref[:, off : off + 2 * BUCKET, :].astype(F32).reshape(PEERS, 2, BUCKET, LANES)
        return both[:, 0].reshape(n, LANES), both[:, 1].reshape(n, LANES)

    def put(pair, h, a, b):
        off = (pair * HPD + h) * 2 * BUCKET
        both = jnp.concatenate(
            [a.reshape(PEERS, BUCKET, LANES), b.reshape(PEERS, BUCKET, LANES)], axis=1
        ).astype(BF16)
        out_ref[:, pl.ds(pl.multiple_of(i * BLOCK + off, 16), 2 * BUCKET), :] = both

    value_grads = []
    for h in range(HPD):
        q, k = pair_of(0, h)
        v, g = pair_of(1, h)
        q, k, g = q.astype(BF16), k.astype(BF16), g.astype(BF16)
        v = (v + extra[:, h * LANES : (h + 1) * LANES]).astype(BF16)
        s = dot_nt(q, k) * scale + bias
        e = jnp.exp(s - jnp.max(s, axis=1, keepdims=True))
        p = e * (1.0 / jnp.sum(e, axis=1, keepdims=True))
        w = p.astype(BF16)
        out = dot(w, v)
        value_grad = dot_tn(w, g)
        pg = dot_nt(g, v)
        centre = jnp.sum(p * pg, axis=1, keepdims=True)
        sg = (p * (pg - centre)).astype(BF16)
        query_grad = dot(sg, k) * scale
        key_grad = dot_tn(sg, q) * scale
        put(0, h, out, query_grad)
        put(1, h, key_grad, value_grad)
        value_grads.append(value_grad.astype(BF16))

    part = dot_tn(pick, jnp.concatenate(value_grads, axis=1))

    @pl.when(i == 0)
    def _():
        acc_ref[...] = part

    @pl.when(i > 0)
    def _():
        acc_ref[...] += part

    @pl.when(i == OWN - 1)
    def _():
        acc = acc_ref[...]
        high = acc.astype(BF16)
        low = (acc - high.astype(F32)).astype(BF16)
        weight = w_ref[...]
        tg = dot_nt(high, weight) + dot_nt(low, weight)
        tg = tg.reshape(PEERS, BUCKET, TEXT)
        for c in range(2):
            both = jnp.concatenate(
                [tg[:, :, 2 * c * LANES : (2 * c + 1) * LANES], tg[:, :, (2 * c + 1) * LANES : (2 * c + 2) * LANES]],
                axis=1,
            ).astype(BF16)
            off = OWN * BLOCK + c * 2 * BUCKET
            out_ref[:, off : off + 2 * BUCKET, :] = both
        text = text_ref[...]
        wg_ref[...] = dot_tn(text, high) + dot_tn(text, low)


def attend(zi, msg, own, got, w):
    full = lambda shape: pl.BlockSpec(shape, lambda i, z: (0,) * len(shape))
    return pl.pallas_call(
        attend_kernel,
        grid_spec=pltpu.PrefetchScalarGridSpec(
            num_scalar_prefetch=1,
            grid=(OWN,),
            in_specs=[
                full((PEERS * 8, LANES)),
                full((COMPACT, LANES)),
                pl.BlockSpec((PEERS, BLOCK, LANES), lambda i, z: (0, i, 0)),
                pl.BlockSpec((PEERS, TEXT_ROWS, LANES), lambda i, z: (0, OWN * BLOCK // TEXT_ROWS, 0)),
                full((TEXT, COLS)),
            ],
            out_specs=[full((PEERS, MSG_ROWS, LANES)), full((TEXT, COLS))],
            scratch_shapes=[pltpu.VMEM((GTEXT, COLS), F32), pltpu.VMEM((GTEXT, TEXT), BF16)],
        ),
        out_shape=[
            jax.ShapeDtypeStruct((PEERS, MSG_ROWS, LANES), BF16),
            jax.ShapeDtypeStruct((TEXT, COLS), F32),
        ],
        compiler_params=pltpu.CompilerParams(vmem_limit_bytes=24 << 20),
        name="attend",
    )(zi, msg, own, got, got, w)


def unpack_kernel(msg_ref, dest_ref, in_ref, o_ref, q_ref, k_ref, v_ref, tg_ref, sel_ref):
    x = pl.program_id(0)

    @pl.when(x == 0)
    def _():
        _, match = owner_match(msg_ref, dest_ref)
        sel_ref[...] = jnp.transpose(bucket_select(match)).astype(BF16)

    sel = sel_ref[...]
    for pair, (a_ref, b_ref) in enumerate(((o_ref, q_ref), (k_ref, v_ref))):
        for h in range(HPD):
            parts = []
            for i in range(OWN):
                off = i * BLOCK + (pair * HPD + h) * 2 * BUCKET
                parts.append(
                    in_ref[:, 0, off : off + 2 * BUCKET, :].astype(F32).reshape(NZ, 1, 2, BUCKET, LANES)
                )
            both = jnp.concatenate(parts, axis=1)
            a = both[:, :, 0].reshape(COMPACT * BUCKET, LANES).astype(BF16)
            b = both[:, :, 1].reshape(COMPACT * BUCKET, LANES).astype(BF16)
            span = slice(h * LANES, (h + 1) * LANES)
            a_ref[:, span] = dot(sel, a).astype(BF16)
            b_ref[:, span] = dot(sel, b).astype(BF16)

    for c in range(2):
        off = OWN * BLOCK + c * 2 * BUCKET
        total = jnp.sum(in_ref[:, 0, off : off + 2 * BUCKET, :].astype(F32), axis=0)
        for half in range(2):
            span = slice((2 * c + half) * LANES, (2 * c + half + 1) * LANES)
            piece = total[half * BUCKET : (half + 1) * BUCKET]

            @pl.when(x == 0)
            def _():
                tg_ref[:, span] = piece

            @pl.when(x > 0)
            def _():
                tg_ref[:, span] += piece


def unpack(msg, dest, got):
    full = lambda shape: pl.BlockSpec(shape, lambda x: (0,) * len(shape))
    cols = pl.BlockSpec((ROWS, COLS), lambda x: (0, x))
    rows = jax.ShapeDtypeStruct((ROWS, NX * COLS), BF16)
    return pl.pallas_call(
        unpack_kernel,
        grid=(NX,),
        in_specs=[
            full((PEERS * 8, LANES)),
            full((1, LANES)),
            pl.BlockSpec((NZ, 1, MSG_ROWS, LANES), lambda x: (0, x, 0, 0)),
        ],
        out_specs=[cols, cols, cols, cols, full((BUCKET, TEXT))],
        out_shape=[rows, rows, rows, rows, jax.ShapeDtypeStruct((BUCKET, TEXT), F32)],
        scratch_shapes=[pltpu.VMEM((ROWS, COMPACT * BUCKET), BF16)],
        compiler_params=pltpu.CompilerParams(vmem_limit_bytes=24 << 20),
        name="unpack",
    )(msg, dest, got)


def exchange(x):
    return lax.all_to_all(x, "seq", split_axis=0, concat_axis=0, tiled=True)


def swap(x, axis, bit):
    size = lax.axis_size(axis)
    return lax.ppermute(x, axis, [(j, j ^ bit) for j in range(size)])


def gather_bits(x, axis, bits):
    index = lax.axis_index(axis)
    for depth, bit in enumerate(bits):
        other = swap(x, axis, bit)
        up = (index & bit) != 0
        first = jnp.where(up, other, x)
        second = jnp.where(up, x, other)
        x = jnp.stack([first, second], axis=depth)
    return x


def halve(x, axis, bit, dim):
    up = (lax.axis_index(axis) & bit) != 0
    zero, one = lax.index_in_dim(x, 0, dim, False), lax.index_in_dim(x, 1, dim, False)
    return jnp.where(up, one, zero) + swap(jnp.where(up, zero, one), axis, bit)


def x_split_kernel(x_ref, in_ref, *out_refs):
    for f, out_ref in enumerate(out_refs):
        for j in range(NZ):
            out_ref[pl.ds(j, 1), :] = in_ref[pl.ds(j * NX + (x_ref[0] ^ f), 1), :]


def z_split_kernel(z_ref, *refs):
    for f, out_ref in enumerate(refs[NX:]):
        for j in range(NX):
            out_ref[pl.ds(j, 1), :] = refs[j][pl.ds(z_ref[0] ^ f, 1), :]


def row_sum_kernel(x_ref, *refs):
    out_ref, total_ref = refs[NZ:]
    total = refs[0][...]
    for f in range(1, NZ):
        total = total + refs[f][...]
    total_ref[...] = total
    for c in range(NX):
        out_ref[:, c * COLS : (c + 1) * COLS] = total_ref[pl.ds(x_ref[0] ^ c, 1), :]


def small_call(kernel, outs, scratch, index, *args):
    return pl.pallas_call(
        kernel,
        out_shape=[jax.ShapeDtypeStruct(shape, F32) for shape in outs],
        in_specs=[pl.BlockSpec(memory_space=pltpu.SMEM)]
        + [pl.BlockSpec(memory_space=pltpu.VMEM)] * len(args),
        scratch_shapes=scratch,
        compiler_params=pltpu.CompilerParams(vmem_limit_bytes=4 << 20),
    )(index, *args)


def reduce_weight(wg, zi, xi):
    wg = wg.reshape(2, 2, 2, 2, PEERS, COLS)
    wg = halve(wg, "dp", 1, 3)
    for bit, dim in ((2, 2), (4, 1), (8, 0)):
        wg = halve(wg, "dp", bit, dim)
    parts = small_call(x_split_kernel, [(NZ, COLS)] * NX, [], xi, wg)
    parts = [parts[0]] + [swap(parts[f], "seq", f) for f in range(1, NX)]
    parts = small_call(z_split_kernel, [(NX, COLS)] * NZ, [], zi, *parts)
    parts = [parts[0]] + [swap(parts[f], "seq", f * NX) for f in range(1, NZ)]
    return small_call(row_sum_kernel, [(1, NX * COLS)], [pltpu.VMEM((NX, COLS), F32)], xi, *parts)[0]


def local(query, key, value, text, cond_weight, cotangent, dest, segment, align):
    seq = lax.axis_index("seq").astype(jnp.int32)
    zi = (seq >> 2).reshape(1)
    xi = (seq & 3).reshape(1)
    dest_row = dest.reshape(1, ROWS)
    first = prep(dest_row, align.reshape(1, ROWS), segment.reshape(1, SLOTS), cond_weight)
    msg3 = exchange(first.reshape(PEERS, 8, LANES))
    msg = msg3.reshape(PEERS * 8, LANES)
    packed, own = pack(msg, dest_row, text, query, key, value, cotangent)
    got = exchange(packed.reshape(PEERS, MSG_ROWS, LANES))
    my_w = msg3[:, 4 : 4 + HPD, :].astype(BF16).reshape(PEERS, COLS)
    full_w = gather_bits(my_w, "dp", (8, 4, 2, 1)).reshape(TEXT, COLS)
    back, wg = attend(zi, msg, own, got, full_w)
    returned = exchange(back)
    weight_grad = reduce_weight(wg, zi, xi)
    attended, query_grad, key_grad, value_grad, text_grad = unpack(
        msg, dest_row, returned.reshape(NZ, NX, MSG_ROWS, LANES)
    )
    return attended, query_grad, key_grad, value_grad, text_grad, weight_grad


def solution(mesh):
    rows = P(("dp", "seq"), None)
    flat = P(("dp", "seq"))
    return jax.shard_map(
        local,
        mesh=mesh,
        in_specs=(rows, rows, rows, rows, rows, rows, flat, flat, flat),
        out_specs=(rows,) * 6,
        check_vma=False,
    )
```

```python
import jax
import jax.numpy as jnp
from jax import lax
from jax.experimental import pallas as pl
from jax.experimental.pallas import tpu as pltpu
from jax.sharding import PartitionSpec as P

F32 = jnp.float32
BF16 = jnp.bfloat16

NZ, NX = 8, 4
PEERS = NZ * NX
ROWS = 128
SLOTS = 256
BUCKET = 8
OWN = 3
HPD = 3
COMPACT = NZ * OWN
LANES = 128
COLS = HPD * LANES
TEXT = 512
GTEXT = 256
BLOCK = 2 * HPD * 2 * BUCKET
TEXT_ROWS = 32
MSG_ROWS = OWN * BLOCK + TEXT_ROWS


def iota(shape, dim):
    return lax.broadcasted_iota(jnp.int32, shape, dim)


def dot(a, b):
    return jnp.dot(a, b, preferred_element_type=F32)


def dot_nt(a, b):
    return lax.dot_general(a, b, (((1,), (1,)), ((), ())), preferred_element_type=F32)


def dot_tn(a, b):
    return lax.dot_general(a, b, (((0,), (0,)), ((), ())), preferred_element_type=F32)


def upper(n):
    return (iota((n, n), 0) <= iota((n, n), 1)).astype(BF16)


def spread8(x):
    n = x.shape[0]
    return jnp.broadcast_to(x[:, None, :], (n, BUCKET, LANES)).reshape(n * BUCKET, LANES)


def bucket_select(match):
    n = match.shape[0]
    count = dot(match.astype(BF16), upper(ROWS))
    rank = ((iota((n * BUCKET, LANES), 0) & (BUCKET - 1)) + 1).astype(F32)
    hit = (spread8(count) == rank) & (spread8(match) > 0.5)
    return jnp.where(hit, 1.0, 0.0)


def compact_owners(seg_first):
    flag = jnp.where(jnp.broadcast_to(seg_first[:, 0:1], (PEERS, LANES)) >= 0.0, 1.0, 0.0)
    lower = (iota((PEERS, PEERS), 0) >= iota((PEERS, PEERS), 1)).astype(BF16)
    count = dot(lower, flag.astype(BF16))
    lane = (iota((PEERS, LANES), 1) + 1).astype(F32)
    hit = jnp.where((count == lane) & (flag > 0.5), 1.0, 0.0)
    ids = iota((PEERS, LANES), 0).astype(F32) + 1.0
    row = jnp.sum(hit * ids, axis=0, keepdims=True) - 1.0
    diag = iota((COMPACT, LANES), 0) == iota((COMPACT, LANES), 1)
    col = jnp.sum(jnp.where(diag, jnp.broadcast_to(row, (COMPACT, LANES)), 0.0), axis=1, keepdims=True)
    return jnp.broadcast_to(col, (COMPACT, LANES))


def prep_kernel(dest_ref, align_ref, seg_ref, w_ref, out_ref):
    sub = iota((8, LANES), 0)

    def row(v):
        return jnp.broadcast_to(v.astype(F32), (8, LANES))

    base = jnp.where(sub == 0, row(dest_ref[...]), 0.0)
    base = jnp.where(sub == 1, row(align_ref[...]), base)
    seg = seg_ref[...]
    base = jnp.where(sub == 2, row(seg[:, :LANES]), base)
    base = jnp.where(sub == 3, row(seg[:, LANES:]), base)
    w = w_ref[...].astype(F32)
    for x in range(NX):
        msg = base
        for h in range(HPD):
            start = (x * HPD + h) * LANES
            msg = jnp.where(sub == 4 + h, row(w[:, start : start + LANES]), msg)
        for z in range(NZ):
            out_ref[z, x] = msg


def prep(dest, align, seg, w):
    return pl.pallas_call(
        prep_kernel,
        out_shape=jax.ShapeDtypeStruct((NZ, NX, 8, LANES), F32),
        name="prep",
    )(dest, align, seg, w)


def owner_match(msg_ref, dest_ref):
    owners = compact_owners(msg_ref[pl.ds(2, PEERS, stride=8), :])
    mine = jnp.broadcast_to(dest_ref[...] >> 8, (COMPACT, LANES)).astype(F32)
    return owners, jnp.where(mine == owners, 1.0, 0.0)


def pack_kernel(msg_ref, dest_ref, text_ref, q_ref, k_ref, v_ref, g_ref, out_ref, own_ref, sel_ref):
    @pl.when(pl.program_id(0) == 0)
    def _():
        owners, match = owner_match(msg_ref, dest_ref)
        own_ref[...] = owners
        sel_ref[...] = bucket_select(match).astype(BF16)

    sel = sel_ref[...]
    for pair, (a_ref, b_ref) in enumerate(((q_ref, k_ref), (v_ref, g_ref))):
        a = dot(sel, a_ref[...]).reshape(COMPACT, BUCKET, COLS)
        b = dot(sel, b_ref[...]).reshape(COMPACT, BUCKET, COLS)
        both = jnp.concatenate([a, b], axis=1).astype(BF16).reshape(NZ, OWN, 2 * BUCKET, COLS)
        for i in range(OWN):
            for h in range(HPD):
                off = i * BLOCK + (pair * HPD + h) * 2 * BUCKET
                out_ref[:, 0, off : off + 2 * BUCKET, :] = both[:, i, :, h * LANES : (h + 1) * LANES]
    text = text_ref[...].astype(F32)
    for c in range(2):
        tile = jnp.concatenate(
            [text[:, 2 * c * LANES : (2 * c + 1) * LANES], text[:, (2 * c + 1) * LANES : (2 * c + 2) * LANES]], axis=0
        ).astype(BF16)
        off = OWN * BLOCK + c * 2 * BUCKET
        for z in range(NZ):
            out_ref[z, 0, off : off + 2 * BUCKET, :] = tile


def pack(msg, dest, text, q, k, v, g):
    full = lambda shape: pl.BlockSpec(shape, lambda x: (0,) * len(shape))
    cols = pl.BlockSpec((ROWS, COLS), lambda x: (0, x))
    return pl.pallas_call(
        pack_kernel,
        grid=(NX,),
        in_specs=[full((PEERS * 8, LANES)), full((1, LANES)), full((BUCKET, TEXT)), cols, cols, cols, cols],
        out_specs=[
            pl.BlockSpec((NZ, 1, MSG_ROWS, LANES), lambda x: (0, x, 0, 0)),
            full((COMPACT, LANES)),
        ],
        out_shape=[
            jax.ShapeDtypeStruct((NZ, NX, MSG_ROWS, LANES), BF16),
            jax.ShapeDtypeStruct((COMPACT, LANES), F32),
        ],
        scratch_shapes=[pltpu.VMEM((COMPACT * BUCKET, LANES), BF16)],
        name="pack",
    )(msg, dest, text, q, k, v, g)


def attend_kernel(z_ref, msg_ref, own_ref, in_ref, tail_ref, w_ref, out_ref, wg_ref, acc_ref, text_ref):
    i = pl.program_id(0)
    n = SLOTS

    @pl.when(i < OWN)
    def _():

        owner = jnp.broadcast_to(own_ref[pl.ds(z_ref[0] * OWN + i, 1), :], (PEERS, LANES))
        dest = msg_ref[pl.ds(0, PEERS, stride=8), :].astype(jnp.int32)
        match = jnp.where((dest >> 8).astype(F32) == owner, 1.0, 0.0)
        sel = bucket_select(match)
        valid = jnp.sum(sel, axis=1, keepdims=True)
        slot = jnp.sum(sel * spread8((dest & (SLOTS - 1)).astype(F32)), axis=1, keepdims=True)
        slot = jnp.where(valid > 0.5, slot, -1.0)
        align = jnp.sum(sel * spread8(msg_ref[pl.ds(1, PEERS, stride=8), :]), axis=1, keepdims=True)
        align = jnp.where(valid > 0.5, align, -1.0)

        mine = iota((PEERS, LANES), 0).astype(F32) == owner
        seg_lo = jnp.sum(jnp.where(mine, msg_ref[pl.ds(2, PEERS, stride=8), :], 0.0), axis=0, keepdims=True)
        seg_hi = jnp.sum(jnp.where(mine, msg_ref[pl.ds(3, PEERS, stride=8), :], 0.0), axis=0, keepdims=True)
        seg = jnp.concatenate([seg_lo, seg_hi], axis=1)
        lane = iota((n, n), 1)
        lanef = lane.astype(F32)
        diag = iota((n, n), 0) == lane
        label = jnp.sum(jnp.where(lanef == slot, jnp.broadcast_to(seg, (n, n)), 0.0), axis=1, keepdims=True)
        label = jnp.where(valid > 0.5, label, -1.0)
        label_b = jnp.broadcast_to(label, (n, n))
        label_row = jnp.sum(jnp.where(diag, label_b, 0.0), axis=0, keepdims=True)
        allowed = ((label_b == jnp.broadcast_to(label_row, (n, n))) & (label_b >= 0.0)) | diag
        bias = jnp.where(allowed, 0.0, -1e30)

        @pl.when(i == 0)
        def _():
            for c in range(2):
                tiles = tail_ref[:, c * 2 * BUCKET : (c + 1) * 2 * BUCKET, :].astype(F32)
                tiles = tiles.reshape(PEERS, 2, BUCKET, LANES)
                for half in range(2):
                    span = slice((2 * c + half) * LANES, (2 * c + half + 1) * LANES)
                    text_ref[:, span] = tiles[:, half].reshape(GTEXT, LANES).astype(BF16)

        pick = jnp.where(lanef == align, 1.0, 0.0).astype(BF16)
        cond = dot(pick, text_ref[...]).astype(BF16)
        extra = dot(cond, w_ref[...])

        scale = LANES ** (-0.5)

        def pair_of(pair, h):
            off = (pair * HPD + h) * 2 * BUCKET
            both = in_ref[:, off : off + 2 * BUCKET, :].astype(F32).reshape(PEERS, 2, BUCKET, LANES)
            return both[:, 0].reshape(n, LANES), both[:, 1].reshape(n, LANES)

        def put(pair, h, a, b):
            off = (pair * HPD + h) * 2 * BUCKET
            both = jnp.concatenate(
                [a.reshape(PEERS, BUCKET, LANES), b.reshape(PEERS, BUCKET, LANES)], axis=1
            ).astype(BF16)
            out_ref[:, off : off + 2 * BUCKET, :] = both

        value_grads = []
        for h in range(HPD):
            q, k = pair_of(0, h)
            v, g = pair_of(1, h)
            q, k, g = q.astype(BF16), k.astype(BF16), g.astype(BF16)
            v = (v + extra[:, h * LANES : (h + 1) * LANES]).astype(BF16)
            s = dot_nt(q, k) * scale + bias
            e = jnp.exp(s - jnp.max(s, axis=1, keepdims=True))
            p = e * (1.0 / jnp.sum(e, axis=1, keepdims=True))
            w = p.astype(BF16)
            out = dot(w, v)
            value_grad = dot_tn(w, g)
            pg = dot_nt(g, v)
            centre = jnp.sum(p * pg, axis=1, keepdims=True)
            sg = (p * (pg - centre)).astype(BF16)
            query_grad = dot(sg, k) * scale
            key_grad = dot_tn(sg, q) * scale
            put(0, h, out, query_grad)
            put(1, h, key_grad, value_grad)
            value_grads.append(value_grad.astype(BF16))

        part = dot_tn(pick, jnp.concatenate(value_grads, axis=1))

        @pl.when(i == 0)
        def _():
            acc_ref[...] = part

        @pl.when(i > 0)
        def _():
            acc_ref[...] += part

    @pl.when(i == OWN)
    def _():
        acc = acc_ref[...]
        high = acc.astype(BF16)
        low = (acc - high.astype(F32)).astype(BF16)
        weight = w_ref[...]
        tg = dot_nt(high, weight) + dot_nt(low, weight)
        tg = tg.reshape(PEERS, BUCKET, TEXT)
        for c in range(2):
            both = jnp.concatenate(
                [tg[:, :, 2 * c * LANES : (2 * c + 1) * LANES], tg[:, :, (2 * c + 1) * LANES : (2 * c + 2) * LANES]],
                axis=1,
            ).astype(BF16)
            off = c * 2 * BUCKET
            out_ref[:, off : off + 2 * BUCKET, :] = both
        text = text_ref[...]
        wg_ref[...] = dot_tn(text, high) + dot_tn(text, low)


def attend(zi, msg, own, got, w):
    full = lambda shape: pl.BlockSpec(shape, lambda i, z: (0,) * len(shape))
    return pl.pallas_call(
        attend_kernel,
        grid_spec=pltpu.PrefetchScalarGridSpec(
            num_scalar_prefetch=1,
            grid=(OWN + 1,),
            in_specs=[
                full((PEERS * 8, LANES)),
                full((COMPACT, LANES)),
                pl.BlockSpec((PEERS, BLOCK, LANES), lambda i, z: (0, jnp.minimum(i, OWN - 1), 0)),
                pl.BlockSpec((PEERS, TEXT_ROWS, LANES), lambda i, z: (0, OWN * BLOCK // TEXT_ROWS, 0)),
                full((TEXT, COLS)),
            ],
            out_specs=[pl.BlockSpec((PEERS, BLOCK, LANES), lambda i, z: (0, i, 0)), full((TEXT, COLS))],
            scratch_shapes=[pltpu.VMEM((GTEXT, COLS), F32), pltpu.VMEM((GTEXT, TEXT), BF16)],
        ),
        out_shape=[
            pltpu.HBM((PEERS, MSG_ROWS, LANES), BF16),
            jax.ShapeDtypeStruct((TEXT, COLS), F32),
        ],
        compiler_params=pltpu.CompilerParams(vmem_limit_bytes=24 << 20),
        name="attend",
    )(zi, msg, own, got, got, w)


def unpack_kernel(msg_ref, dest_ref, in_ref, o_ref, q_ref, k_ref, v_ref, tg_ref, sel_ref):
    x = pl.program_id(0)

    @pl.when(x == 0)
    def _():
        _, match = owner_match(msg_ref, dest_ref)
        sel_ref[...] = jnp.transpose(bucket_select(match)).astype(BF16)

    sel = sel_ref[...]
    for pair, (a_ref, b_ref) in enumerate(((o_ref, q_ref), (k_ref, v_ref))):
        for h in range(HPD):
            parts = []
            for i in range(OWN):
                off = i * BLOCK + (pair * HPD + h) * 2 * BUCKET
                parts.append(
                    in_ref[:, 0, off : off + 2 * BUCKET, :].astype(F32).reshape(NZ, 1, 2, BUCKET, LANES)
                )
            both = jnp.concatenate(parts, axis=1)
            a = both[:, :, 0].reshape(COMPACT * BUCKET, LANES).astype(BF16)
            b = both[:, :, 1].reshape(COMPACT * BUCKET, LANES).astype(BF16)
            span = slice(h * LANES, (h + 1) * LANES)
            a_ref[:, span] = dot(sel, a).astype(BF16)
            b_ref[:, span] = dot(sel, b).astype(BF16)

    for c in range(2):
        off = OWN * BLOCK + c * 2 * BUCKET
        total = jnp.sum(in_ref[:, 0, off : off + 2 * BUCKET, :].astype(F32), axis=0)
        for half in range(2):
            span = slice((2 * c + half) * LANES, (2 * c + half + 1) * LANES)
            piece = total[half * BUCKET : (half + 1) * BUCKET]

            @pl.when(x == 0)
            def _():
                tg_ref[:, span] = piece

            @pl.when(x > 0)
            def _():
                tg_ref[:, span] += piece


def unpack(msg, dest, got):
    full = lambda shape: pl.BlockSpec(shape, lambda x: (0,) * len(shape))
    cols = pl.BlockSpec((ROWS, COLS), lambda x: (0, x))
    rows = jax.ShapeDtypeStruct((ROWS, NX * COLS), BF16)
    return pl.pallas_call(
        unpack_kernel,
        grid=(NX,),
        in_specs=[
            full((PEERS * 8, LANES)),
            full((1, LANES)),
            pl.BlockSpec((NZ, 1, MSG_ROWS, LANES), lambda x: (0, x, 0, 0)),
        ],
        out_specs=[cols, cols, cols, cols, full((BUCKET, TEXT))],
        out_shape=[rows, rows, rows, rows, jax.ShapeDtypeStruct((BUCKET, TEXT), F32)],
        scratch_shapes=[pltpu.VMEM((ROWS, COMPACT * BUCKET), BF16)],
        compiler_params=pltpu.CompilerParams(vmem_limit_bytes=24 << 20),
        name="unpack",
    )(msg, dest, got)


def exchange(x):
    return lax.all_to_all(x, "seq", split_axis=0, concat_axis=0, tiled=True)


def swap(x, axis, bit):
    size = lax.axis_size(axis)
    return lax.ppermute(x, axis, [(j, j ^ bit) for j in range(size)])


def gather_bits(x, axis, bits):
    index = lax.axis_index(axis)
    for depth, bit in enumerate(bits):
        other = swap(x, axis, bit)
        up = (index & bit) != 0
        first = jnp.where(up, other, x)
        second = jnp.where(up, x, other)
        x = jnp.stack([first, second], axis=depth)
    return x


def halve(x, axis, bit, dim, kind):
    up = (lax.axis_index(axis) & bit) != 0
    zero, one = lax.index_in_dim(x, 0, dim, False), lax.index_in_dim(x, 1, dim, False)
    return jnp.where(up, one, zero), swap(jnp.where(up, zero, one).astype(kind), axis, bit)


def y_split_kernel(y_ref, keep_ref, got_ref, own_ref, *send_refs):
    for h in range(2):
        for f, out_ref in enumerate((own_ref,) + send_refs):
            j = h * 4 + (y_ref[0] ^ f)
            out_ref[h] = (keep_ref[j] + got_ref[j].astype(F32)).astype(out_ref.dtype)


def x_split_kernel(x_ref, keep_ref, got_ref, *refs):
    total_ref = refs[NX]
    total_ref[...] = keep_ref[...] + got_ref[...].astype(F32)
    for f, out_ref in enumerate(refs[:NX]):
        for j in range(NZ):
            out_ref[pl.ds(j, 1), :] = total_ref[pl.ds(j * NX + (x_ref[0] ^ f), 1), :]


def z_split_kernel(z_ref, *refs):
    low = z_ref[0] & 3
    for f, out_ref in enumerate(refs[NX:]):
        for h in range(2):
            for j in range(NX):
                out_ref[pl.ds(h * NX + j, 1), :] = refs[j][pl.ds(h * 4 + (low ^ f), 1), :]


def row_sum_kernel(x_ref, keep_ref, got_ref, out_ref, total_ref):
    total_ref[...] = keep_ref[...] + got_ref[...]
    for c in range(NX):
        out_ref[:, c * COLS : (c + 1) * COLS] = total_ref[pl.ds(x_ref[0] ^ c, 1), :]


def small_call(kernel, outs, scratch, index, *args):
    return pl.pallas_call(
        kernel,
        out_shape=[jax.ShapeDtypeStruct(shape, kind) for shape, kind in outs],
        in_specs=[pl.BlockSpec(memory_space=pltpu.SMEM)]
        + [pl.BlockSpec(memory_space=pltpu.VMEM)] * len(args),
        scratch_shapes=scratch,
        compiler_params=pltpu.CompilerParams(vmem_limit_bytes=8 << 20),
    )(index, *args)


def reduce_weight(wg, zi, xi):
    wg = wg.reshape(8, 2, PEERS, COLS)
    keep, got = halve(wg, "dp", 1, 1, BF16)
    yi = ((lax.axis_index("dp").astype(jnp.int32) >> 1) & 3).reshape(1)
    half = (2, PEERS, COLS)
    parts = small_call(y_split_kernel, [(half, F32)] + [(half, BF16)] * 3, [], yi, keep, got)
    total = parts[0]
    for f in range(1, 4):
        total = total + swap(parts[f], "dp", 2 * f).astype(F32)
    keep, got = halve(total, "dp", 8, 0, BF16)
    piece = ((NZ, COLS), F32)
    parts = small_call(x_split_kernel, [piece] * NX, [pltpu.VMEM((PEERS, COLS), F32)], xi, keep, got)
    parts = [parts[0]] + [swap(parts[f], "seq", f) for f in range(1, NX)]
    parts = small_call(z_split_kernel, [piece] * 4, [], zi, *parts)
    total = parts[0]
    for f in range(1, 4):
        total = total + swap(parts[f], "seq", f * NX)
    keep, got = halve(total.reshape(2, NX, COLS), "seq", 16, 0, F32)
    row = [((1, NX * COLS), F32)]
    return small_call(row_sum_kernel, row, [pltpu.VMEM((NX, COLS), F32)], xi, keep, got)[0]


def local(query, key, value, text, cond_weight, cotangent, dest, segment, align):
    seq = lax.axis_index("seq").astype(jnp.int32)
    zi = (seq >> 2).reshape(1)
    xi = (seq & 3).reshape(1)
    dest_row = dest.reshape(1, ROWS)
    first = prep(dest_row, align.reshape(1, ROWS), segment.reshape(1, SLOTS), cond_weight)
    msg3 = exchange(first.reshape(PEERS, 8, LANES))
    msg = msg3.reshape(PEERS * 8, LANES)
    packed, own = pack(msg, dest_row, text, query, key, value, cotangent)
    got = exchange(packed.reshape(PEERS, MSG_ROWS, LANES))
    my_w = msg3[:, 4 : 4 + HPD, :].astype(BF16).reshape(PEERS, COLS)
    full_w = gather_bits(my_w, "dp", (8, 4, 2, 1)).reshape(TEXT, COLS)
    back, wg = attend(zi, msg, own, got, full_w)
    returned = exchange(back)
    weight_grad = reduce_weight(wg, zi, xi)
    attended, query_grad, key_grad, value_grad, text_grad = unpack(
        msg, dest_row, returned.reshape(NZ, NX, MSG_ROWS, LANES)
    )
    return attended, query_grad, key_grad, value_grad, text_grad, weight_grad


def solution(mesh):
    rows = P(("dp", "seq"), None)
    flat = P(("dp", "seq"))
    return jax.shard_map(
        local,
        mesh=mesh,
        in_specs=(rows, rows, rows, rows, rows, rows, flat, flat, flat),
        out_specs=(rows,) * 6,
        check_vma=False,
    )
```

```python
import jax
import jax.numpy as jnp
from jax import lax
from jax.experimental import pallas as pl
from jax.experimental.pallas import tpu as pltpu
from jax.sharding import PartitionSpec as P

F32 = jnp.float32
BF16 = jnp.bfloat16

NZ, NX = 8, 4
PEERS = NZ * NX
ROWS = 128
SLOTS = 256
BUCKET = 8
OWNERS = 21
HPD = 3
UNITS = 8
COMPACT = 24
NEAR = 4
LANES = 128
COLS = HPD * LANES
TEXT = 512
GTEXT = 256
BLOCK = 2 * 2 * BUCKET
TEXT_ROWS = 32
BODY_ROWS = UNITS * BLOCK
MSG_ROWS = BODY_ROWS + TEXT_ROWS
STEP = 2


def iota(shape, dim):
    return lax.broadcasted_iota(jnp.int32, shape, dim)


def dot(a, b):
    return jnp.dot(a, b, preferred_element_type=F32)


def dot_nt(a, b):
    return lax.dot_general(a, b, (((1,), (1,)), ((), ())), preferred_element_type=F32)


def dot_tn(a, b):
    return lax.dot_general(a, b, (((0,), (0,)), ((), ())), preferred_element_type=F32)


def upper(n):
    return (iota((n, n), 0) <= iota((n, n), 1)).astype(BF16)


def spread8(x):
    n = x.shape[0]
    return jnp.broadcast_to(x[:, None, :], (n, BUCKET, LANES)).reshape(n * BUCKET, LANES)


def bucket_select(match):
    n = match.shape[0]
    count = dot(match.astype(BF16), upper(ROWS))
    rank = ((iota((n * BUCKET, LANES), 0) & (BUCKET - 1)) + 1).astype(F32)
    hit = (spread8(count) == rank) & (spread8(match) > 0.5)
    return jnp.where(hit, 1.0, 0.0)


def compact_owners(seg_first):
    flag = jnp.where(jnp.broadcast_to(seg_first[:, 0:1], (PEERS, LANES)) >= 0.0, 1.0, 0.0)
    lower = (iota((PEERS, PEERS), 0) >= iota((PEERS, PEERS), 1)).astype(BF16)
    count = dot(lower, flag.astype(BF16))
    lane = (iota((PEERS, LANES), 1) + 1).astype(F32)
    hit = jnp.where((count == lane) & (flag > 0.5), 1.0, 0.0)
    ids = iota((PEERS, LANES), 0).astype(F32) + 1.0
    row = jnp.sum(hit * ids, axis=0, keepdims=True) - 1.0
    diag = iota((COMPACT, LANES), 0) == iota((COMPACT, LANES), 1)
    col = jnp.sum(jnp.where(diag, jnp.broadcast_to(row, (COMPACT, LANES)), 0.0), axis=1, keepdims=True)
    return jnp.broadcast_to(col, (COMPACT, LANES))


def prep_kernel(dest_ref, align_ref, seg_ref, w_ref, out_ref):
    sub = iota((8, LANES), 0)

    def row(v):
        return jnp.broadcast_to(v.astype(F32), (8, LANES))

    base = jnp.where(sub == 0, row(dest_ref[...]), 0.0)
    base = jnp.where(sub == 1, row(align_ref[...]), base)
    seg = seg_ref[...]
    base = jnp.where(sub == 2, row(seg[:, :LANES]), base)
    base = jnp.where(sub == 3, row(seg[:, LANES:]), base)
    w = w_ref[...].astype(F32)
    for x in range(NX):
        msg = base
        for h in range(HPD):
            start = (x * HPD + h) * LANES
            msg = jnp.where(sub == 4 + h, row(w[:, start : start + LANES]), msg)
        for z in range(NZ):
            out_ref[z, x] = msg


def prep(dest, align, seg, w):
    return pl.pallas_call(
        prep_kernel,
        out_shape=jax.ShapeDtypeStruct((NZ, NX, 8, LANES), F32),
        name="prep",
    )(dest, align, seg, w)


def owner_match(msg_ref, dest_ref):
    owners = compact_owners(msg_ref[pl.ds(2, PEERS, stride=8), :])
    mine = jnp.broadcast_to(dest_ref[...] >> 8, (COMPACT, LANES)).astype(F32)
    return owners, jnp.where(mine == owners, 1.0, 0.0)


def pack_kernel(msg_ref, dest_ref, text_ref, q_ref, k_ref, v_ref, g_ref, out_ref, own_ref, sel_ref):
    @pl.when(pl.program_id(0) == 0)
    def _():
        owners, match = owner_match(msg_ref, dest_ref)
        own_ref[...] = owners
        sel_ref[...] = bucket_select(match).astype(BF16)

    sel = sel_ref[...]
    for pair, (a_ref, b_ref) in enumerate(((q_ref, k_ref), (v_ref, g_ref))):
        a = dot(sel, a_ref[...]).reshape(COMPACT, BUCKET, COLS)
        b = dot(sel, b_ref[...]).reshape(COMPACT, BUCKET, COLS)
        both = jnp.concatenate([a, b], axis=1).astype(BF16)
        for unit in range(NZ * UNITS):
            owner, h = divmod(unit, HPD)
            off = unit % UNITS * BLOCK + pair * 2 * BUCKET
            out_ref[unit // UNITS, 0, off : off + 2 * BUCKET, :] = both[owner, :, h * LANES : (h + 1) * LANES]
    text = text_ref[...].astype(F32)
    for c in range(2):
        tile = jnp.concatenate(
            [text[:, 2 * c * LANES : (2 * c + 1) * LANES], text[:, (2 * c + 1) * LANES : (2 * c + 2) * LANES]], axis=0
        ).astype(BF16)
        off = BODY_ROWS + c * 2 * BUCKET
        for z in range(NZ):
            out_ref[z, 0, off : off + 2 * BUCKET, :] = tile


def pack(msg, dest, text, q, k, v, g):
    full = lambda shape: pl.BlockSpec(shape, lambda x: (0,) * len(shape))
    cols = pl.BlockSpec((ROWS, COLS), lambda x: (0, x))
    return pl.pallas_call(
        pack_kernel,
        grid=(NX,),
        in_specs=[full((PEERS * 8, LANES)), full((1, LANES)), full((BUCKET, TEXT)), cols, cols, cols, cols],
        out_specs=[
            pl.BlockSpec((NZ, 1, MSG_ROWS, LANES), lambda x: (0, x, 0, 0)),
            full((COMPACT, LANES)),
        ],
        out_shape=[
            jax.ShapeDtypeStruct((NZ, NX, MSG_ROWS, LANES), BF16),
            jax.ShapeDtypeStruct((COMPACT, LANES), F32),
        ],
        scratch_shapes=[pltpu.VMEM((COMPACT * BUCKET, LANES), BF16)],
        name="pack",
    )(msg, dest, text, q, k, v, g)


def owner_setup(owner, msg_ref, text):
    n = SLOTS
    dest = msg_ref[pl.ds(0, PEERS, stride=8), :].astype(jnp.int32)
    match = jnp.where((dest >> 8).astype(F32) == owner, 1.0, 0.0)
    sel = bucket_select(match)
    valid = jnp.sum(sel, axis=1, keepdims=True)
    slot = jnp.sum(sel * spread8((dest & (SLOTS - 1)).astype(F32)), axis=1, keepdims=True)
    slot = jnp.where(valid > 0.5, slot, -1.0)
    align = jnp.sum(sel * spread8(msg_ref[pl.ds(1, PEERS, stride=8), :]), axis=1, keepdims=True)
    align = jnp.where(valid > 0.5, align, -1.0)

    mine = iota((PEERS, LANES), 0).astype(F32) == owner
    seg_lo = jnp.sum(jnp.where(mine, msg_ref[pl.ds(2, PEERS, stride=8), :], 0.0), axis=0, keepdims=True)
    seg_hi = jnp.sum(jnp.where(mine, msg_ref[pl.ds(3, PEERS, stride=8), :], 0.0), axis=0, keepdims=True)
    seg = jnp.concatenate([seg_lo, seg_hi], axis=1)
    lane = iota((n, n), 1)
    lanef = lane.astype(F32)
    diag = iota((n, n), 0) == lane
    label = jnp.sum(jnp.where(lanef == slot, jnp.broadcast_to(seg, (n, n)), 0.0), axis=1, keepdims=True)
    label = jnp.where(valid > 0.5, label, -1.0)
    label_b = jnp.broadcast_to(label, (n, n))
    label_row = jnp.sum(jnp.where(diag, label_b, 0.0), axis=0, keepdims=True)
    allowed = ((label_b == jnp.broadcast_to(label_row, (n, n))) & (label_b >= 0.0)) | diag
    pick = jnp.where(lanef == align, 1.0, 0.0).astype(BF16)
    return jnp.where(allowed, 0.0, -1e30), pick, dot(pick, text).astype(BF16)


def attend_kernel(
    z_ref, msg_ref, own_ref, in_ref, tail_ref, w_ref, out_ref, wg_ref,
    acc_ref, text_ref, w3_ref, bias_ref, pick_ref, cond_ref,
):
    i = pl.program_id(0)
    n = SLOTS
    unit0 = z_ref[0] * UNITS
    owner0 = unit0 // HPD

    @pl.when(i == 0)
    def _():
        for c in range(2):
            tiles = tail_ref[:, c * 2 * BUCKET : (c + 1) * 2 * BUCKET, :].astype(F32)
            tiles = tiles.reshape(PEERS, 2, BUCKET, LANES)
            for half in range(2):
                span = slice((2 * c + half) * LANES, (2 * c + half + 1) * LANES)
                text_ref[:, span] = tiles[:, half].reshape(GTEXT, LANES).astype(BF16)
        text = text_ref[...]
        for t in range(NEAR):
            owner = jnp.broadcast_to(own_ref[pl.ds(owner0 + t, 1), :], (PEERS, LANES))
            bias, pick, cond = owner_setup(owner, msg_ref, text)
            bias_ref[t] = bias
            pick_ref[t] = pick
            cond_ref[t] = cond
        for h in range(HPD):
            w3_ref[h] = w_ref[:, h * LANES : (h + 1) * LANES]
        acc_ref[...] = jnp.zeros_like(acc_ref)

    scale = LANES ** (-0.5)

    @pl.when(i < UNITS // STEP)
    def _():
        for u in range(STEP):
            unit = unit0 + i * STEP + u
            owner = unit // HPD
            h = unit - owner * HPD
            t = owner - owner0

            def pair_of(pair):
                off = u * BLOCK + pair * 2 * BUCKET
                both = in_ref[:, off : off + 2 * BUCKET, :].astype(F32).reshape(PEERS, 2, BUCKET, LANES)
                return both[:, 0].reshape(n, LANES), both[:, 1].reshape(n, LANES)

            def put(pair, a, b):
                off = u * BLOCK + pair * 2 * BUCKET
                out_ref[:, off : off + 2 * BUCKET, :] = jnp.concatenate(
                    [a.reshape(PEERS, BUCKET, LANES), b.reshape(PEERS, BUCKET, LANES)], axis=1
                ).astype(BF16)

            q, k = pair_of(0)
            v, g = pair_of(1)
            q, k, g = q.astype(BF16), k.astype(BF16), g.astype(BF16)
            v = (v + dot(cond_ref[t], w3_ref[h])).astype(BF16)
            s = dot_nt(q, k) * scale + bias_ref[t]
            e = jnp.exp(s - jnp.max(s, axis=1, keepdims=True))
            p = e * (1.0 / jnp.sum(e, axis=1, keepdims=True))
            w = p.astype(BF16)
            out = dot(w, v)
            value_grad = dot_tn(w, g)
            pg = dot_nt(g, v)
            centre = jnp.sum(p * pg, axis=1, keepdims=True)
            sg = (p * (pg - centre)).astype(BF16)
            query_grad = dot(sg, k) * scale
            key_grad = dot_tn(sg, q) * scale
            put(0, out, query_grad)
            put(1, key_grad, value_grad)
            acc_ref[h] += dot_tn(pick_ref[t], value_grad.astype(BF16))

    @pl.when(i == UNITS // STEP)
    def _():
        text = text_ref[...]
        tg = jnp.zeros((GTEXT, TEXT), F32)
        for h in range(HPD):
            acc = acc_ref[h]
            high = acc.astype(BF16)
            low = (acc - high.astype(F32)).astype(BF16)
            tg = tg + dot_nt(high, w3_ref[h]) + dot_nt(low, w3_ref[h])
            wg_ref[:, h * LANES : (h + 1) * LANES] = dot_tn(text, high) + dot_tn(text, low)
        tg = tg.reshape(PEERS, BUCKET, TEXT)
        for c in range(2):
            both = jnp.concatenate(
                [tg[:, :, 2 * c * LANES : (2 * c + 1) * LANES], tg[:, :, (2 * c + 1) * LANES : (2 * c + 2) * LANES]],
                axis=1,
            ).astype(BF16)
            off = c * 2 * BUCKET
            out_ref[:, off : off + 2 * BUCKET, :] = both


def attend(zi, msg, own, got, w):
    full = lambda shape: pl.BlockSpec(shape, lambda i, z: (0,) * len(shape))
    last = UNITS // STEP - 1
    return pl.pallas_call(
        attend_kernel,
        grid_spec=pltpu.PrefetchScalarGridSpec(
            num_scalar_prefetch=1,
            grid=(UNITS // STEP + 1,),
            in_specs=[
                full((PEERS * 8, LANES)),
                full((COMPACT, LANES)),
                pl.BlockSpec((PEERS, STEP * BLOCK, LANES), lambda i, z: (0, jnp.minimum(i, last), 0)),
                pl.BlockSpec((PEERS, TEXT_ROWS, LANES), lambda i, z: (0, BODY_ROWS // TEXT_ROWS, 0)),
                full((TEXT, COLS)),
            ],
            out_specs=[pl.BlockSpec((PEERS, STEP * BLOCK, LANES), lambda i, z: (0, i, 0)), full((TEXT, COLS))],
            scratch_shapes=[
                pltpu.VMEM((HPD, GTEXT, LANES), F32),
                pltpu.VMEM((GTEXT, TEXT), BF16),
                pltpu.VMEM((HPD, TEXT, LANES), BF16),
                pltpu.VMEM((NEAR, SLOTS, SLOTS), F32),
                pltpu.VMEM((NEAR, SLOTS, GTEXT), BF16),
                pltpu.VMEM((NEAR, SLOTS, TEXT), BF16),
            ],
        ),
        out_shape=[
            pltpu.HBM((PEERS, MSG_ROWS, LANES), BF16),
            pltpu.HBM((TEXT, COLS), F32),
        ],
        compiler_params=pltpu.CompilerParams(vmem_limit_bytes=28 << 20),
        name="attend",
    )(zi, msg, own, got, got, w)


def unpack_kernel(msg_ref, dest_ref, in_ref, o_ref, q_ref, k_ref, v_ref, tg_ref, sel_ref):
    x = pl.program_id(0)

    @pl.when(x == 0)
    def _():
        _, match = owner_match(msg_ref, dest_ref)
        sel_ref[...] = jnp.transpose(bucket_select(match)).astype(BF16)

    sel = sel_ref[...]
    for pair, (a_ref, b_ref) in enumerate(((o_ref, q_ref), (k_ref, v_ref))):
        for h in range(HPD):
            tiles = []
            for owner in range(OWNERS):
                unit = owner * HPD + h
                off = unit % UNITS * BLOCK + pair * 2 * BUCKET
                tiles.append(in_ref[unit // UNITS, 0, off : off + 2 * BUCKET, :].astype(F32))
            blank = [jnp.zeros((BUCKET, LANES), F32)] * (COMPACT - OWNERS)
            a = jnp.concatenate([t[:BUCKET] for t in tiles] + blank, axis=0).astype(BF16)
            b = jnp.concatenate([t[BUCKET:] for t in tiles] + blank, axis=0).astype(BF16)
            span = slice(h * LANES, (h + 1) * LANES)
            a_ref[:, span] = dot(sel, a).astype(BF16)
            b_ref[:, span] = dot(sel, b).astype(BF16)

    for c in range(2):
        off = BODY_ROWS + c * 2 * BUCKET
        total = jnp.sum(in_ref[:, 0, off : off + 2 * BUCKET, :].astype(F32), axis=0)
        for half in range(2):
            span = slice((2 * c + half) * LANES, (2 * c + half + 1) * LANES)
            piece = total[half * BUCKET : (half + 1) * BUCKET]

            @pl.when(x == 0)
            def _():
                tg_ref[:, span] = piece

            @pl.when(x > 0)
            def _():
                tg_ref[:, span] += piece


def unpack(msg, dest, got):
    full = lambda shape: pl.BlockSpec(shape, lambda x: (0,) * len(shape))
    cols = pl.BlockSpec((ROWS, COLS), lambda x: (0, x))
    rows = jax.ShapeDtypeStruct((ROWS, NX * COLS), BF16)
    return pl.pallas_call(
        unpack_kernel,
        grid=(NX,),
        in_specs=[
            full((PEERS * 8, LANES)),
            full((1, LANES)),
            pl.BlockSpec((NZ, 1, MSG_ROWS, LANES), lambda x: (0, x, 0, 0)),
        ],
        out_specs=[cols, cols, cols, cols, full((BUCKET, TEXT))],
        out_shape=[rows, rows, rows, rows, jax.ShapeDtypeStruct((BUCKET, TEXT), F32)],
        scratch_shapes=[pltpu.VMEM((ROWS, COMPACT * BUCKET), BF16)],
        compiler_params=pltpu.CompilerParams(vmem_limit_bytes=24 << 20),
        name="unpack",
    )(msg, dest, got)


def exchange(x):
    return lax.all_to_all(x, "seq", split_axis=0, concat_axis=0, tiled=True)


def swap(x, axis, bit):
    size = lax.axis_size(axis)
    return lax.ppermute(x, axis, [(j, j ^ bit) for j in range(size)])


def gather_bits(x, axis, bits):
    index = lax.axis_index(axis)
    for depth, bit in enumerate(bits):
        other = swap(x, axis, bit)
        up = (index & bit) != 0
        first = jnp.where(up, other, x)
        second = jnp.where(up, x, other)
        x = jnp.stack([first, second], axis=depth)
    return x


def halve(x, axis, bit, dim, kind):
    up = (lax.axis_index(axis) & bit) != 0
    zero, one = lax.index_in_dim(x, 0, dim, False), lax.index_in_dim(x, 1, dim, False)
    return jnp.where(up, one, zero), swap(jnp.where(up, zero, one).astype(kind), axis, bit)


def x_split_kernel(x_ref, keep_ref, got_ref, *refs):
    total_ref = refs[NX]
    total_ref[...] = keep_ref[...] + got_ref[...].astype(F32)
    for f, out_ref in enumerate(refs[:NX]):
        for j in range(NZ):
            out_ref[pl.ds(j, 1), :] = total_ref[pl.ds(j * NX + (x_ref[0] ^ f), 1), :]


def z_split_kernel(z_ref, *refs):
    low = z_ref[0] & 3
    for f, out_ref in enumerate(refs[NX:]):
        for h in range(2):
            for j in range(NX):
                out_ref[pl.ds(h * NX + j, 1), :] = refs[j][pl.ds(h * 4 + (low ^ f), 1), :]


def row_sum_kernel(x_ref, keep_ref, got_ref, out_ref, total_ref):
    total_ref[...] = keep_ref[...] + got_ref[...]
    for c in range(NX):
        out_ref[:, c * COLS : (c + 1) * COLS] = total_ref[pl.ds(x_ref[0] ^ c, 1), :]


def small_call(kernel, outs, scratch, index, *args):
    return pl.pallas_call(
        kernel,
        out_shape=[jax.ShapeDtypeStruct(shape, kind) for shape, kind in outs],
        in_specs=[pl.BlockSpec(memory_space=pltpu.SMEM)]
        + [pl.BlockSpec(memory_space=pltpu.VMEM)] * len(args),
        scratch_shapes=scratch,
        compiler_params=pltpu.CompilerParams(vmem_limit_bytes=8 << 20),
    )(index, *args)


def reduce_weight(wg, zi, xi):
    wg = wg.reshape(2, 2, 2, 2, PEERS, COLS)
    keep, got = halve(wg, "dp", 1, 3, BF16)
    for bit, dim in ((2, 2), (4, 1), (8, 0)):
        keep, got = halve(keep + got.astype(F32), "dp", bit, dim, BF16)
    piece = ((NZ, COLS), F32)
    parts = small_call(x_split_kernel, [piece] * NX, [pltpu.VMEM((PEERS, COLS), F32)], xi, keep, got)
    parts = [parts[0]] + [swap(parts[f], "seq", f) for f in range(1, NX)]
    parts = small_call(z_split_kernel, [piece] * 4, [], zi, *parts)
    total = parts[0]
    for f in range(1, 4):
        total = total + swap(parts[f], "seq", f * NX)
    keep, got = halve(total.reshape(2, NX, COLS), "seq", 16, 0, F32)
    row = [((1, NX * COLS), F32)]
    return small_call(row_sum_kernel, row, [pltpu.VMEM((NX, COLS), F32)], xi, keep, got)[0]


def local(query, key, value, text, cond_weight, cotangent, dest, segment, align):
    seq = lax.axis_index("seq").astype(jnp.int32)
    zi = (seq >> 2).reshape(1)
    xi = (seq & 3).reshape(1)
    dest_row = dest.reshape(1, ROWS)
    first = prep(dest_row, align.reshape(1, ROWS), segment.reshape(1, SLOTS), cond_weight)
    msg3 = exchange(first.reshape(PEERS, 8, LANES))
    msg = msg3.reshape(PEERS * 8, LANES)
    packed, own = pack(msg, dest_row, text, query, key, value, cotangent)
    got = exchange(packed.reshape(PEERS, MSG_ROWS, LANES))
    my_w = msg3[:, 4 : 4 + HPD, :].astype(BF16).reshape(PEERS, COLS)
    full_w = gather_bits(my_w, "dp", (8, 4, 2, 1)).reshape(TEXT, COLS)
    back, wg = attend(zi, msg, own, got, full_w)
    returned = exchange(back)
    weight_grad = reduce_weight(wg, zi, xi)
    attended, query_grad, key_grad, value_grad, text_grad = unpack(
        msg, dest_row, returned.reshape(NZ, NX, MSG_ROWS, LANES)
    )
    return attended, query_grad, key_grad, value_grad, text_grad, weight_grad


def solution(mesh):
    rows = P(("dp", "seq"), None)
    flat = P(("dp", "seq"))
    return jax.shard_map(
        local,
        mesh=mesh,
        in_specs=(rows, rows, rows, rows, rows, rows, flat, flat, flat),
        out_specs=(rows,) * 6,
        check_vma=False,
    )
```

```python
import jax
import jax.numpy as jnp
from jax import lax
from jax.experimental import pallas as pl
from jax.experimental.pallas import tpu as pltpu
from jax.sharding import PartitionSpec as P

F32 = jnp.float32
BF16 = jnp.bfloat16

NZ, NX = 8, 4
PEERS = NZ * NX
ROWS = 128
SLOTS = 256
BUCKET = 8
OWNERS = 21
HPD = 3
UNITS = 8
COMPACT = 24
NEAR = 4
LANES = 128
COLS = HPD * LANES
TEXT = 512
GTEXT = 256
BLOCK = 2 * 2 * BUCKET
TEXT_ROWS = 32
BODY_ROWS = UNITS * BLOCK
MSG_ROWS = BODY_ROWS + TEXT_ROWS
STEP = 2


def iota(shape, dim):
    return lax.broadcasted_iota(jnp.int32, shape, dim)


def dot(a, b):
    return jnp.dot(a, b, preferred_element_type=F32)


def dot_nt(a, b):
    return lax.dot_general(a, b, (((1,), (1,)), ((), ())), preferred_element_type=F32)


def dot_tn(a, b):
    return lax.dot_general(a, b, (((0,), (0,)), ((), ())), preferred_element_type=F32)


def upper(n):
    return (iota((n, n), 0) <= iota((n, n), 1)).astype(BF16)


def spread8(x):
    n = x.shape[0]
    return jnp.broadcast_to(x[:, None, :], (n, BUCKET, LANES)).reshape(n * BUCKET, LANES)


def bucket_select(match):
    n = match.shape[0]
    count = dot(match.astype(BF16), upper(ROWS))
    rank = ((iota((n * BUCKET, LANES), 0) & (BUCKET - 1)) + 1).astype(F32)
    hit = (spread8(count) == rank) & (spread8(match) > 0.5)
    return jnp.where(hit, 1.0, 0.0)


def compact_owners(seg_first):
    flag = jnp.where(jnp.broadcast_to(seg_first[:, 0:1], (PEERS, LANES)) >= 0.0, 1.0, 0.0)
    lower = (iota((PEERS, PEERS), 0) >= iota((PEERS, PEERS), 1)).astype(BF16)
    count = dot(lower, flag.astype(BF16))
    lane = (iota((PEERS, LANES), 1) + 1).astype(F32)
    hit = jnp.where((count == lane) & (flag > 0.5), 1.0, 0.0)
    ids = iota((PEERS, LANES), 0).astype(F32) + 1.0
    row = jnp.sum(hit * ids, axis=0, keepdims=True) - 1.0
    diag = iota((COMPACT, LANES), 0) == iota((COMPACT, LANES), 1)
    col = jnp.sum(jnp.where(diag, jnp.broadcast_to(row, (COMPACT, LANES)), 0.0), axis=1, keepdims=True)
    return jnp.broadcast_to(col, (COMPACT, LANES))


def prep_kernel(dest_ref, align_ref, seg_ref, w_ref, out_ref):
    sub = iota((8, LANES), 0)

    def row(v):
        return jnp.broadcast_to(v.astype(F32), (8, LANES))

    base = jnp.where(sub == 0, row(dest_ref[...]), 0.0)
    base = jnp.where(sub == 1, row(align_ref[...]), base)
    seg = seg_ref[...]
    base = jnp.where(sub == 2, row(seg[:, :LANES]), base)
    base = jnp.where(sub == 3, row(seg[:, LANES:]), base)
    w = w_ref[...].astype(F32)
    for x in range(NX):
        msg = base
        for h in range(HPD):
            start = (x * HPD + h) * LANES
            msg = jnp.where(sub == 4 + h, row(w[:, start : start + LANES]), msg)
        for z in range(NZ):
            out_ref[z, x] = msg


def prep(dest, align, seg, w):
    return pl.pallas_call(
        prep_kernel,
        out_shape=jax.ShapeDtypeStruct((NZ, NX, 8, LANES), F32),
        name="prep",
    )(dest, align, seg, w)


def owner_match(msg_ref, dest_ref):
    owners = compact_owners(msg_ref[pl.ds(2, PEERS, stride=8), :])
    mine = jnp.broadcast_to(dest_ref[...] >> 8, (COMPACT, LANES)).astype(F32)
    return owners, jnp.where(mine == owners, 1.0, 0.0)


def pack_kernel(msg_ref, dest_ref, text_ref, q_ref, k_ref, v_ref, g_ref, out_ref, own_ref, sel_ref):
    @pl.when(pl.program_id(0) == 0)
    def _():
        owners, match = owner_match(msg_ref, dest_ref)
        own_ref[...] = owners
        sel_ref[...] = bucket_select(match).astype(BF16)

    sel = sel_ref[...]
    for pair, (a_ref, b_ref) in enumerate(((q_ref, k_ref), (v_ref, g_ref))):
        a = dot(sel, a_ref[...]).reshape(COMPACT, BUCKET, COLS)
        b = dot(sel, b_ref[...]).reshape(COMPACT, BUCKET, COLS)
        both = jnp.concatenate([a, b], axis=1).astype(BF16)
        for unit in range(NZ * UNITS):
            owner, h = divmod(unit, HPD)
            off = unit % UNITS * BLOCK + pair * 2 * BUCKET
            out_ref[unit // UNITS, 0, off : off + 2 * BUCKET, :] = both[owner, :, h * LANES : (h + 1) * LANES]
    text = text_ref[...].astype(F32)
    for c in range(2):
        tile = jnp.concatenate(
            [text[:, 2 * c * LANES : (2 * c + 1) * LANES], text[:, (2 * c + 1) * LANES : (2 * c + 2) * LANES]], axis=0
        ).astype(BF16)
        off = BODY_ROWS + c * 2 * BUCKET
        for z in range(NZ):
            out_ref[z, 0, off : off + 2 * BUCKET, :] = tile


def pack(msg, dest, text, q, k, v, g):
    full = lambda shape: pl.BlockSpec(shape, lambda x: (0,) * len(shape))
    cols = pl.BlockSpec((ROWS, COLS), lambda x: (0, x))
    return pl.pallas_call(
        pack_kernel,
        grid=(NX,),
        in_specs=[full((PEERS * 8, LANES)), full((1, LANES)), full((BUCKET, TEXT)), cols, cols, cols, cols],
        out_specs=[
            pl.BlockSpec((NZ, 1, MSG_ROWS, LANES), lambda x: (0, x, 0, 0)),
            full((COMPACT, LANES)),
        ],
        out_shape=[
            jax.ShapeDtypeStruct((NZ, NX, MSG_ROWS, LANES), BF16),
            jax.ShapeDtypeStruct((COMPACT, LANES), F32),
        ],
        scratch_shapes=[pltpu.VMEM((COMPACT * BUCKET, LANES), BF16)],
        name="pack",
    )(msg, dest, text, q, k, v, g)


def owner_setup(owner, msg_ref):
    n = SLOTS
    dest = msg_ref[pl.ds(0, PEERS, stride=8), :].astype(jnp.int32)
    match = jnp.where((dest >> 8).astype(F32) == owner, 1.0, 0.0)
    sel = bucket_select(match)
    valid = jnp.sum(sel, axis=1, keepdims=True)
    slot = jnp.sum(sel * spread8((dest & (SLOTS - 1)).astype(F32)), axis=1, keepdims=True)
    slot = jnp.where(valid > 0.5, slot, -1.0)
    align = jnp.sum(sel * spread8(msg_ref[pl.ds(1, PEERS, stride=8), :]), axis=1, keepdims=True)
    align = jnp.where(valid > 0.5, align, -1.0)

    mine = iota((PEERS, LANES), 0).astype(F32) == owner
    seg_lo = jnp.sum(jnp.where(mine, msg_ref[pl.ds(2, PEERS, stride=8), :], 0.0), axis=0, keepdims=True)
    seg_hi = jnp.sum(jnp.where(mine, msg_ref[pl.ds(3, PEERS, stride=8), :], 0.0), axis=0, keepdims=True)
    seg = jnp.concatenate([seg_lo, seg_hi], axis=1)
    lane = iota((n, n), 1)
    lanef = lane.astype(F32)
    diag = iota((n, n), 0) == lane
    label = jnp.sum(jnp.where(lanef == slot, jnp.broadcast_to(seg, (n, n)), 0.0), axis=1, keepdims=True)
    label = jnp.where(valid > 0.5, label, -1.0)
    label_b = jnp.broadcast_to(label, (n, n))
    label_row = jnp.sum(jnp.where(diag, label_b, 0.0), axis=0, keepdims=True)
    allowed = ((label_b == jnp.broadcast_to(label_row, (n, n))) & (label_b >= 0.0)) | diag
    pick = jnp.where(lanef == align, 1.0, 0.0).astype(BF16)
    return jnp.where(allowed, 0.0, -1e30), pick


def setup_kernel(z_ref, msg_ref, own_ref, bias_ref, pick_ref):
    owner0 = z_ref[0] * UNITS // HPD
    for t in range(NEAR):
        owner = jnp.broadcast_to(own_ref[pl.ds(owner0 + t, 1), :], (PEERS, LANES))
        bias_ref[t], pick_ref[t] = owner_setup(owner, msg_ref)


def setup(zi, msg, own):
    return pl.pallas_call(
        setup_kernel,
        in_specs=[pl.BlockSpec(memory_space=pltpu.SMEM)] + [pl.BlockSpec(memory_space=pltpu.VMEM)] * 2,
        out_shape=[
            pltpu.HBM((NEAR, SLOTS, SLOTS), F32),
            pltpu.HBM((NEAR, SLOTS, GTEXT), BF16),
        ],
        compiler_params=pltpu.CompilerParams(vmem_limit_bytes=24 << 20),
        name="setup",
    )(zi, msg, own)


def attend_kernel(
    z_ref, bias_ref, pick_ref, in_ref, tail_ref, w_ref, out_ref, wg_ref, acc_ref, text_ref, w3_ref, cond_ref
):
    i = pl.program_id(0)
    n = SLOTS
    unit0 = z_ref[0] * UNITS
    owner0 = unit0 // HPD

    @pl.when(i == 0)
    def _():
        for c in range(2):
            tiles = tail_ref[:, c * 2 * BUCKET : (c + 1) * 2 * BUCKET, :].astype(F32)
            tiles = tiles.reshape(PEERS, 2, BUCKET, LANES)
            for half in range(2):
                span = slice((2 * c + half) * LANES, (2 * c + half + 1) * LANES)
                text_ref[:, span] = tiles[:, half].reshape(GTEXT, LANES).astype(BF16)
        text = text_ref[...]
        for t in range(NEAR):
            cond_ref[t] = dot(pick_ref[t], text).astype(BF16)
        for h in range(HPD):
            w3_ref[h] = w_ref[:, h * LANES : (h + 1) * LANES]
        acc_ref[...] = jnp.zeros_like(acc_ref)

    scale = LANES ** (-0.5)

    @pl.when(i < UNITS // STEP)
    def _():
        for u in range(STEP):
            unit = unit0 + i * STEP + u
            owner = unit // HPD
            h = unit - owner * HPD
            t = owner - owner0

            def pair_of(pair):
                off = u * BLOCK + pair * 2 * BUCKET
                both = in_ref[:, off : off + 2 * BUCKET, :].astype(F32).reshape(PEERS, 2, BUCKET, LANES)
                return both[:, 0].reshape(n, LANES), both[:, 1].reshape(n, LANES)

            def put(pair, a, b):
                off = u * BLOCK + pair * 2 * BUCKET
                out_ref[:, off : off + 2 * BUCKET, :] = jnp.concatenate(
                    [a.reshape(PEERS, BUCKET, LANES), b.reshape(PEERS, BUCKET, LANES)], axis=1
                ).astype(BF16)

            q, k = pair_of(0)
            v, g = pair_of(1)
            q, k, g = q.astype(BF16), k.astype(BF16), g.astype(BF16)
            v = (v + dot(cond_ref[t], w3_ref[h])).astype(BF16)
            s = dot_nt(q, k) * scale + bias_ref[t]
            e = jnp.exp(s - jnp.max(s, axis=1, keepdims=True))
            p = e * (1.0 / jnp.sum(e, axis=1, keepdims=True))
            w = p.astype(BF16)
            out = dot(w, v)
            value_grad = dot_tn(w, g)
            pg = dot_nt(g, v)
            centre = jnp.sum(p * pg, axis=1, keepdims=True)
            sg = (p * (pg - centre)).astype(BF16)
            query_grad = dot(sg, k) * scale
            key_grad = dot_tn(sg, q) * scale
            put(0, out, query_grad)
            put(1, key_grad, value_grad)
            acc_ref[h] += dot_tn(pick_ref[t], value_grad.astype(BF16))

    @pl.when(i == UNITS // STEP)
    def _():
        text = text_ref[...]
        tg = jnp.zeros((GTEXT, TEXT), F32)
        for h in range(HPD):
            acc = acc_ref[h]
            high = acc.astype(BF16)
            low = (acc - high.astype(F32)).astype(BF16)
            tg = tg + dot_nt(high, w3_ref[h]) + dot_nt(low, w3_ref[h])
            wg_ref[:, h * LANES : (h + 1) * LANES] = dot_tn(text, high) + dot_tn(text, low)
        tg = tg.reshape(PEERS, BUCKET, TEXT)
        for c in range(2):
            both = jnp.concatenate(
                [tg[:, :, 2 * c * LANES : (2 * c + 1) * LANES], tg[:, :, (2 * c + 1) * LANES : (2 * c + 2) * LANES]],
                axis=1,
            ).astype(BF16)
            off = c * 2 * BUCKET
            out_ref[:, off : off + 2 * BUCKET, :] = both


def attend(zi, bias, pick, got, w):
    full = lambda shape: pl.BlockSpec(shape, lambda i, z: (0,) * len(shape))
    last = UNITS // STEP - 1
    return pl.pallas_call(
        attend_kernel,
        grid_spec=pltpu.PrefetchScalarGridSpec(
            num_scalar_prefetch=1,
            grid=(UNITS // STEP + 1,),
            in_specs=[
                full((NEAR, SLOTS, SLOTS)),
                full((NEAR, SLOTS, GTEXT)),
                pl.BlockSpec((PEERS, STEP * BLOCK, LANES), lambda i, z: (0, jnp.minimum(i, last), 0)),
                pl.BlockSpec((PEERS, TEXT_ROWS, LANES), lambda i, z: (0, BODY_ROWS // TEXT_ROWS, 0)),
                full((TEXT, COLS)),
            ],
            out_specs=[pl.BlockSpec((PEERS, STEP * BLOCK, LANES), lambda i, z: (0, i, 0)), full((TEXT, COLS))],
            scratch_shapes=[
                pltpu.VMEM((HPD, GTEXT, LANES), F32),
                pltpu.VMEM((GTEXT, TEXT), BF16),
                pltpu.VMEM((HPD, TEXT, LANES), BF16),
                pltpu.VMEM((NEAR, SLOTS, TEXT), BF16),
            ],
        ),
        out_shape=[
            pltpu.HBM((PEERS, MSG_ROWS, LANES), BF16),
            pltpu.HBM((TEXT, COLS), F32),
        ],
        compiler_params=pltpu.CompilerParams(vmem_limit_bytes=28 << 20),
        name="attend",
    )(zi, bias, pick, got, got, w)


def unpack_kernel(msg_ref, dest_ref, in_ref, o_ref, q_ref, k_ref, v_ref, tg_ref, sel_ref):
    x = pl.program_id(0)

    @pl.when(x == 0)
    def _():
        _, match = owner_match(msg_ref, dest_ref)
        sel_ref[...] = jnp.transpose(bucket_select(match)).astype(BF16)

    sel = sel_ref[...]
    for pair, (a_ref, b_ref) in enumerate(((o_ref, q_ref), (k_ref, v_ref))):
        for h in range(HPD):
            tiles = []
            for owner in range(OWNERS):
                unit = owner * HPD + h
                off = unit % UNITS * BLOCK + pair * 2 * BUCKET
                tiles.append(in_ref[unit // UNITS, 0, off : off + 2 * BUCKET, :].astype(F32))
            blank = [jnp.zeros((BUCKET, LANES), F32)] * (COMPACT - OWNERS)
            a = jnp.concatenate([t[:BUCKET] for t in tiles] + blank, axis=0).astype(BF16)
            b = jnp.concatenate([t[BUCKET:] for t in tiles] + blank, axis=0).astype(BF16)
            span = slice(h * LANES, (h + 1) * LANES)
            a_ref[:, span] = dot(sel, a).astype(BF16)
            b_ref[:, span] = dot(sel, b).astype(BF16)

    for c in range(2):
        off = BODY_ROWS + c * 2 * BUCKET
        total = jnp.sum(in_ref[:, 0, off : off + 2 * BUCKET, :].astype(F32), axis=0)
        for half in range(2):
            span = slice((2 * c + half) * LANES, (2 * c + half + 1) * LANES)
            piece = total[half * BUCKET : (half + 1) * BUCKET]

            @pl.when(x == 0)
            def _():
                tg_ref[:, span] = piece

            @pl.when(x > 0)
            def _():
                tg_ref[:, span] += piece


def unpack(msg, dest, got):
    full = lambda shape: pl.BlockSpec(shape, lambda x: (0,) * len(shape))
    cols = pl.BlockSpec((ROWS, COLS), lambda x: (0, x))
    rows = jax.ShapeDtypeStruct((ROWS, NX * COLS), BF16)
    return pl.pallas_call(
        unpack_kernel,
        grid=(NX,),
        in_specs=[
            full((PEERS * 8, LANES)),
            full((1, LANES)),
            pl.BlockSpec((NZ, 1, MSG_ROWS, LANES), lambda x: (0, x, 0, 0)),
        ],
        out_specs=[cols, cols, cols, cols, full((BUCKET, TEXT))],
        out_shape=[rows, rows, rows, rows, jax.ShapeDtypeStruct((BUCKET, TEXT), F32)],
        scratch_shapes=[pltpu.VMEM((ROWS, COMPACT * BUCKET), BF16)],
        compiler_params=pltpu.CompilerParams(vmem_limit_bytes=24 << 20),
        name="unpack",
    )(msg, dest, got)


def exchange(x):
    return lax.all_to_all(x, "seq", split_axis=0, concat_axis=0, tiled=True)


def swap(x, axis, bit):
    size = lax.axis_size(axis)
    return lax.ppermute(x, axis, [(j, j ^ bit) for j in range(size)])


def gather_bits(x, axis, bits):
    index = lax.axis_index(axis)
    for depth, bit in enumerate(bits):
        other = swap(x, axis, bit)
        up = (index & bit) != 0
        first = jnp.where(up, other, x)
        second = jnp.where(up, x, other)
        x = jnp.stack([first, second], axis=depth)
    return x


def halve(x, axis, bit, dim, kind):
    up = (lax.axis_index(axis) & bit) != 0
    zero, one = lax.index_in_dim(x, 0, dim, False), lax.index_in_dim(x, 1, dim, False)
    return jnp.where(up, one, zero), swap(jnp.where(up, zero, one).astype(kind), axis, bit)


def x_split_kernel(x_ref, keep_ref, got_ref, *refs):
    total_ref = refs[NX]
    total_ref[...] = keep_ref[...] + got_ref[...].astype(F32)
    for f, out_ref in enumerate(refs[:NX]):
        for j in range(NZ):
            out_ref[pl.ds(j, 1), :] = total_ref[pl.ds(j * NX + (x_ref[0] ^ f), 1), :]


def join_kernel(x_ref, *refs):
    out_ref = refs[NX]
    for z in range(NZ):
        for f in range(NX):
            out_ref[z, pl.ds(f, 1), :] = refs[f][pl.ds(z, 1), :]


def row_sum_kernel(x_ref, in_ref, out_ref, total_ref):
    total = in_ref[0]
    for z in range(1, NZ):
        total = total + in_ref[z]
    total_ref[...] = total
    for c in range(NX):
        out_ref[:, c * COLS : (c + 1) * COLS] = total_ref[pl.ds(x_ref[0] ^ c, 1), :]


def small_call(kernel, outs, scratch, index, *args):
    return pl.pallas_call(
        kernel,
        out_shape=[jax.ShapeDtypeStruct(shape, kind) for shape, kind in outs],
        in_specs=[pl.BlockSpec(memory_space=pltpu.SMEM)]
        + [pl.BlockSpec(memory_space=pltpu.VMEM)] * len(args),
        scratch_shapes=scratch,
        compiler_params=pltpu.CompilerParams(vmem_limit_bytes=8 << 20),
    )(index, *args)


def reduce_weight(wg, xi):
    wg = wg.reshape(2, 2, 2, 2, PEERS, COLS)
    keep, got = halve(wg, "dp", 1, 3, BF16)
    for bit, dim in ((2, 2), (4, 1), (8, 0)):
        keep, got = halve(keep + got.astype(F32), "dp", bit, dim, BF16)
    piece = ((NZ, COLS), F32)
    parts = small_call(x_split_kernel, [piece] * NX, [pltpu.VMEM((PEERS, COLS), F32)], xi, keep, got)
    parts = [parts[0]] + [swap(parts[f], "seq", f) for f in range(1, NX)]
    lines = small_call(join_kernel, [((NZ, NX, COLS), F32)], [], xi, *parts)[0]
    groups = [[z * NX + x for z in range(NZ)] for x in range(NX)]
    lines = lax.all_to_all(lines, "seq", 0, 0, axis_index_groups=groups, tiled=True)
    row = [((1, NX * COLS), F32)]
    return small_call(row_sum_kernel, row, [pltpu.VMEM((NX, COLS), F32)], xi, lines)[0]


def local(query, key, value, text, cond_weight, cotangent, dest, segment, align):
    seq = lax.axis_index("seq").astype(jnp.int32)
    zi = (seq >> 2).reshape(1)
    xi = (seq & 3).reshape(1)
    dest_row = dest.reshape(1, ROWS)
    first = prep(dest_row, align.reshape(1, ROWS), segment.reshape(1, SLOTS), cond_weight)
    msg3 = exchange(first.reshape(PEERS, 8, LANES))
    msg = msg3.reshape(PEERS * 8, LANES)
    packed, own = pack(msg, dest_row, text, query, key, value, cotangent)
    got = exchange(packed.reshape(PEERS, MSG_ROWS, LANES))
    bias, pick = setup(zi, msg, own)
    my_w = msg3[:, 4 : 4 + HPD, :].astype(BF16).reshape(PEERS, COLS)
    full_w = gather_bits(my_w, "dp", (8, 4, 2, 1)).reshape(TEXT, COLS)
    back, wg = attend(zi, bias, pick, got, full_w)
    returned = exchange(back)
    weight_grad = reduce_weight(wg, xi)
    attended, query_grad, key_grad, value_grad, text_grad = unpack(
        msg, dest_row, returned.reshape(NZ, NX, MSG_ROWS, LANES)
    )
    return attended, query_grad, key_grad, value_grad, text_grad, weight_grad


def solution(mesh):
    rows = P(("dp", "seq"), None)
    flat = P(("dp", "seq"))
    return jax.shard_map(
        local,
        mesh=mesh,
        in_specs=(rows, rows, rows, rows, rows, rows, flat, flat, flat),
        out_specs=(rows,) * 6,
        check_vma=False,
    )
```

```python
import jax
import jax.numpy as jnp
from jax import lax
from jax.experimental import pallas as pl
from jax.experimental.pallas import tpu as pltpu
from jax.sharding import PartitionSpec as P

F32 = jnp.float32
BF16 = jnp.bfloat16

NZ, NX = 8, 4
PEERS = NZ * NX
ROWS = 128
SLOTS = 256
BUCKET = 8
OWNERS = 21
HPD = 3
UNITS = 8
COMPACT = 24
NEAR = 4
LANES = 128
COLS = HPD * LANES
TEXT = 512
GTEXT = 256
BLOCK = 2 * 2 * BUCKET
TEXT_ROWS = 32
BODY_ROWS = UNITS * BLOCK
MSG_ROWS = BODY_ROWS + TEXT_ROWS
STEP = 4


def iota(shape, dim):
    return lax.broadcasted_iota(jnp.int32, shape, dim)


def dot(a, b):
    return jnp.dot(a, b, preferred_element_type=F32)


def dot_nt(a, b):
    return lax.dot_general(a, b, (((1,), (1,)), ((), ())), preferred_element_type=F32)


def dot_tn(a, b):
    return lax.dot_general(a, b, (((0,), (0,)), ((), ())), preferred_element_type=F32)


def upper(n):
    return (iota((n, n), 0) <= iota((n, n), 1)).astype(BF16)


def spread8(x):
    n = x.shape[0]
    return jnp.broadcast_to(x[:, None, :], (n, BUCKET, LANES)).reshape(n * BUCKET, LANES)


def bucket_select(match):
    n = match.shape[0]
    count = dot(match.astype(BF16), upper(ROWS))
    rank = ((iota((n * BUCKET, LANES), 0) & (BUCKET - 1)) + 1).astype(F32)
    hit = (spread8(count) == rank) & (spread8(match) > 0.5)
    return jnp.where(hit, 1.0, 0.0)


def compact_owners(seg_first):
    flag = jnp.where(jnp.broadcast_to(seg_first[:, 0:1], (PEERS, LANES)) >= 0.0, 1.0, 0.0)
    lower = (iota((PEERS, PEERS), 0) >= iota((PEERS, PEERS), 1)).astype(BF16)
    count = dot(lower, flag.astype(BF16))
    lane = (iota((PEERS, LANES), 1) + 1).astype(F32)
    hit = jnp.where((count == lane) & (flag > 0.5), 1.0, 0.0)
    ids = iota((PEERS, LANES), 0).astype(F32) + 1.0
    row = jnp.sum(hit * ids, axis=0, keepdims=True) - 1.0
    diag = iota((COMPACT, LANES), 0) == iota((COMPACT, LANES), 1)
    col = jnp.sum(jnp.where(diag, jnp.broadcast_to(row, (COMPACT, LANES)), 0.0), axis=1, keepdims=True)
    return jnp.broadcast_to(col, (COMPACT, LANES))


def prep_kernel(dest_ref, align_ref, seg_ref, w_ref, out_ref):
    sub = iota((8, LANES), 0)

    def row(v):
        return jnp.broadcast_to(v.astype(F32), (8, LANES))

    base = jnp.where(sub == 0, row(dest_ref[...]), 0.0)
    base = jnp.where(sub == 1, row(align_ref[...]), base)
    seg = seg_ref[...]
    base = jnp.where(sub == 2, row(seg[:, :LANES]), base)
    base = jnp.where(sub == 3, row(seg[:, LANES:]), base)
    w = w_ref[...].astype(F32)
    for x in range(NX):
        msg = base
        for h in range(HPD):
            start = (x * HPD + h) * LANES
            msg = jnp.where(sub == 4 + h, row(w[:, start : start + LANES]), msg)
        for z in range(NZ):
            out_ref[z, x] = msg


def prep(dest, align, seg, w):
    return pl.pallas_call(
        prep_kernel,
        out_shape=jax.ShapeDtypeStruct((NZ, NX, 8, LANES), F32),
        name="prep",
    )(dest, align, seg, w)


def owner_match(msg_ref, dest_ref):
    owners = compact_owners(msg_ref[pl.ds(2, PEERS, stride=8), :])
    mine = jnp.broadcast_to(dest_ref[...] >> 8, (COMPACT, LANES)).astype(F32)
    return owners, jnp.where(mine == owners, 1.0, 0.0)


def pack_kernel(msg_ref, dest_ref, text_ref, q_ref, k_ref, v_ref, g_ref, out_ref, own_ref, sel_ref):
    @pl.when(pl.program_id(0) == 0)
    def _():
        owners, match = owner_match(msg_ref, dest_ref)
        own_ref[...] = owners
        sel_ref[...] = bucket_select(match).astype(BF16)

    sel = sel_ref[...]
    for pair, (a_ref, b_ref) in enumerate(((q_ref, k_ref), (v_ref, g_ref))):
        a = dot(sel, a_ref[...]).reshape(COMPACT, BUCKET, COLS)
        b = dot(sel, b_ref[...]).reshape(COMPACT, BUCKET, COLS)
        both = jnp.concatenate([a, b], axis=1).astype(BF16)
        for unit in range(NZ * UNITS):
            owner, h = divmod(unit, HPD)
            off = unit % UNITS * BLOCK + pair * 2 * BUCKET
            out_ref[unit // UNITS, 0, off : off + 2 * BUCKET, :] = both[owner, :, h * LANES : (h + 1) * LANES]
    text = text_ref[...].astype(F32)
    for c in range(2):
        tile = jnp.concatenate(
            [text[:, 2 * c * LANES : (2 * c + 1) * LANES], text[:, (2 * c + 1) * LANES : (2 * c + 2) * LANES]], axis=0
        ).astype(BF16)
        off = BODY_ROWS + c * 2 * BUCKET
        for z in range(NZ):
            out_ref[z, 0, off : off + 2 * BUCKET, :] = tile


def pack(msg, dest, text, q, k, v, g):
    full = lambda shape: pl.BlockSpec(shape, lambda x: (0,) * len(shape))
    cols = pl.BlockSpec((ROWS, COLS), lambda x: (0, x))
    return pl.pallas_call(
        pack_kernel,
        grid=(NX,),
        in_specs=[full((PEERS * 8, LANES)), full((1, LANES)), full((BUCKET, TEXT)), cols, cols, cols, cols],
        out_specs=[
            pl.BlockSpec((NZ, 1, MSG_ROWS, LANES), lambda x: (0, x, 0, 0)),
            full((COMPACT, LANES)),
        ],
        out_shape=[
            jax.ShapeDtypeStruct((NZ, NX, MSG_ROWS, LANES), BF16),
            jax.ShapeDtypeStruct((COMPACT, LANES), F32),
        ],
        scratch_shapes=[pltpu.VMEM((COMPACT * BUCKET, LANES), BF16)],
        name="pack",
    )(msg, dest, text, q, k, v, g)


def owner_setup(owner, msg_ref):
    n = SLOTS
    dest = msg_ref[pl.ds(0, PEERS, stride=8), :].astype(jnp.int32)
    match = jnp.where((dest >> 8).astype(F32) == owner, 1.0, 0.0)
    sel = bucket_select(match)
    valid = jnp.sum(sel, axis=1, keepdims=True)
    slot = jnp.sum(sel * spread8((dest & (SLOTS - 1)).astype(F32)), axis=1, keepdims=True)
    slot = jnp.where(valid > 0.5, slot, -1.0)
    align = jnp.sum(sel * spread8(msg_ref[pl.ds(1, PEERS, stride=8), :]), axis=1, keepdims=True)
    align = jnp.where(valid > 0.5, align, -1.0)

    mine = iota((PEERS, LANES), 0).astype(F32) == owner
    seg_lo = jnp.sum(jnp.where(mine, msg_ref[pl.ds(2, PEERS, stride=8), :], 0.0), axis=0, keepdims=True)
    seg_hi = jnp.sum(jnp.where(mine, msg_ref[pl.ds(3, PEERS, stride=8), :], 0.0), axis=0, keepdims=True)
    seg = jnp.concatenate([seg_lo, seg_hi], axis=1)
    lane = iota((n, n), 1)
    lanef = lane.astype(F32)
    diag = iota((n, n), 0) == lane
    label = jnp.sum(jnp.where(lanef == slot, jnp.broadcast_to(seg, (n, n)), 0.0), axis=1, keepdims=True)
    label = jnp.where(valid > 0.5, label, -1.0)
    label_b = jnp.broadcast_to(label, (n, n))
    label_row = jnp.sum(jnp.where(diag, label_b, 0.0), axis=0, keepdims=True)
    allowed = ((label_b == jnp.broadcast_to(label_row, (n, n))) & (label_b >= 0.0)) | diag
    pick = jnp.where(lanef == align, 1.0, 0.0).astype(BF16)
    return jnp.where(allowed, 0.0, -1e30), pick


def setup_kernel(z_ref, msg_ref, own_ref, bias_ref, pick_ref):
    owner0 = z_ref[0] * UNITS // HPD
    for t in range(NEAR):
        owner = jnp.broadcast_to(own_ref[pl.ds(owner0 + t, 1), :], (PEERS, LANES))
        bias_ref[t], pick_ref[t] = owner_setup(owner, msg_ref)


def setup(zi, msg, own):
    return pl.pallas_call(
        setup_kernel,
        in_specs=[pl.BlockSpec(memory_space=pltpu.SMEM)] + [pl.BlockSpec(memory_space=pltpu.VMEM)] * 2,
        out_shape=[
            pltpu.HBM((NEAR, SLOTS, SLOTS), F32),
            pltpu.HBM((NEAR, SLOTS, GTEXT), BF16),
        ],
        compiler_params=pltpu.CompilerParams(vmem_limit_bytes=24 << 20),
        name="setup",
    )(zi, msg, own)


def attend_kernel(
    z_ref, mask_ref, pick_ref, in_ref, tail_ref, w_ref, out_ref, wg_ref,
    acc_ref, text_ref, w3_ref, cond_ref, bias_ref, bias_sem,
):
    i = pl.program_id(0)
    n = SLOTS
    unit0 = z_ref[0] * UNITS
    owner0 = unit0 // HPD

    @pl.when(i == 0)
    def _():
        copy = pltpu.make_async_copy(mask_ref, bias_ref, bias_sem)
        copy.start()
        for c in range(2):
            tiles = tail_ref[:, c * 2 * BUCKET : (c + 1) * 2 * BUCKET, :].astype(F32)
            tiles = tiles.reshape(PEERS, 2, BUCKET, LANES)
            for half in range(2):
                span = slice((2 * c + half) * LANES, (2 * c + half + 1) * LANES)
                text_ref[:, span] = tiles[:, half].reshape(GTEXT, LANES).astype(BF16)
        text = text_ref[...]
        for t in range(NEAR):
            cond_ref[t] = dot(pick_ref[t], text).astype(BF16)
        for h in range(HPD):
            w3_ref[h] = w_ref[:, h * LANES : (h + 1) * LANES]
        acc_ref[...] = jnp.zeros_like(acc_ref)
        copy.wait()

    scale = LANES ** (-0.5)

    @pl.when(i < UNITS // STEP)
    def _():
        units = range(STEP)
        heads, owners = [], []
        for u in units:
            unit = unit0 + i * STEP + u
            owner = unit // HPD
            heads.append(unit - owner * HPD)
            owners.append(owner - owner0)

        def pair_of(u, pair):
            off = u * BLOCK + pair * 2 * BUCKET
            both = in_ref[:, off : off + 2 * BUCKET, :].astype(F32).reshape(PEERS, 2, BUCKET, LANES)
            return both[:, 0].reshape(n, LANES), both[:, 1].reshape(n, LANES)

        def put(u, pair, a, b):
            off = u * BLOCK + pair * 2 * BUCKET
            out_ref[:, off : off + 2 * BUCKET, :] = jnp.concatenate(
                [a.reshape(PEERS, BUCKET, LANES), b.reshape(PEERS, BUCKET, LANES)], axis=1
            ).astype(BF16)

        qk = [[x.astype(BF16) for x in pair_of(u, 0)] for u in units]
        scores = [dot_nt(q, k) for q, k in qk]
        vg = []
        for u in units:
            v, g = pair_of(u, 1)
            extra = dot(cond_ref[owners[u]], w3_ref[heads[u]])
            vg.append(((v + extra).astype(BF16), g.astype(BF16)))
        prob_grads = [dot_nt(g, v) for v, g in vg]
        probs = []
        for u in units:
            s = scores[u] * scale + bias_ref[owners[u]]
            e = jnp.exp(s - jnp.max(s, axis=1, keepdims=True))
            probs.append(e * (1.0 / jnp.sum(e, axis=1, keepdims=True)))
        weights = [p.astype(BF16) for p in probs]
        score_grads = []
        for p, pg in zip(probs, prob_grads):
            centre = jnp.sum(p * pg, axis=1, keepdims=True)
            score_grads.append((p * (pg - centre)).astype(BF16))
        for u in units:
            (q, k), (v, g) = qk[u], vg[u]
            out = dot(weights[u], v)
            value_grad = dot_tn(weights[u], g)
            query_grad = dot(score_grads[u], k) * scale
            key_grad = dot_tn(score_grads[u], q) * scale
            put(u, 0, out, query_grad)
            put(u, 1, key_grad, value_grad)
            acc_ref[heads[u]] += dot_tn(pick_ref[owners[u]], value_grad.astype(BF16))

    @pl.when(i == UNITS // STEP)
    def _():
        text = text_ref[...]
        tg = jnp.zeros((GTEXT, TEXT), F32)
        for h in range(HPD):
            acc = acc_ref[h].astype(BF16)
            tg = tg + dot_nt(acc, w3_ref[h])
            wg_ref[:, h * LANES : (h + 1) * LANES] = dot_tn(text, acc)
        tg = tg.reshape(PEERS, BUCKET, TEXT)
        for c in range(2):
            both = jnp.concatenate(
                [tg[:, :, 2 * c * LANES : (2 * c + 1) * LANES], tg[:, :, (2 * c + 1) * LANES : (2 * c + 2) * LANES]],
                axis=1,
            ).astype(BF16)
            off = c * 2 * BUCKET
            out_ref[:, off : off + 2 * BUCKET, :] = both


def attend(zi, bias, pick, got, w):
    full = lambda shape: pl.BlockSpec(shape, lambda i, z: (0,) * len(shape))
    last = UNITS // STEP - 1
    return pl.pallas_call(
        attend_kernel,
        grid_spec=pltpu.PrefetchScalarGridSpec(
            num_scalar_prefetch=1,
            grid=(UNITS // STEP + 1,),
            in_specs=[
                pl.BlockSpec(memory_space=pltpu.HBM),
                full((NEAR, SLOTS, GTEXT)),
                pl.BlockSpec((PEERS, STEP * BLOCK, LANES), lambda i, z: (0, jnp.minimum(i, last), 0)),
                pl.BlockSpec((PEERS, TEXT_ROWS, LANES), lambda i, z: (0, BODY_ROWS // TEXT_ROWS, 0)),
                full((TEXT, COLS)),
            ],
            out_specs=[pl.BlockSpec((PEERS, STEP * BLOCK, LANES), lambda i, z: (0, i, 0)), full((TEXT, COLS))],
            scratch_shapes=[
                pltpu.VMEM((HPD, GTEXT, LANES), F32),
                pltpu.VMEM((GTEXT, TEXT), BF16),
                pltpu.VMEM((HPD, TEXT, LANES), BF16),
                pltpu.VMEM((NEAR, SLOTS, TEXT), BF16),
                pltpu.VMEM((NEAR, SLOTS, SLOTS), F32),
                pltpu.SemaphoreType.DMA,
            ],
        ),
        out_shape=[
            pltpu.HBM((PEERS, MSG_ROWS, LANES), BF16),
            pltpu.HBM((TEXT, COLS), F32),
        ],
        compiler_params=pltpu.CompilerParams(vmem_limit_bytes=28 << 20),
        name="attend",
    )(zi, pltpu.with_memory_space_constraint(bias, pltpu.HBM), pick, got, got, w)


def unpack_kernel(msg_ref, dest_ref, in_ref, o_ref, q_ref, k_ref, v_ref, tg_ref, sel_ref):
    x = pl.program_id(0)

    @pl.when(x == 0)
    def _():
        _, match = owner_match(msg_ref, dest_ref)
        sel_ref[...] = jnp.transpose(bucket_select(match)).astype(BF16)

    sel = sel_ref[...]
    for pair, (a_ref, b_ref) in enumerate(((o_ref, q_ref), (k_ref, v_ref))):
        for h in range(HPD):
            tiles = []
            for owner in range(OWNERS):
                unit = owner * HPD + h
                off = unit % UNITS * BLOCK + pair * 2 * BUCKET
                tiles.append(in_ref[unit // UNITS, 0, off : off + 2 * BUCKET, :].astype(F32))
            blank = [jnp.zeros((BUCKET, LANES), F32)] * (COMPACT - OWNERS)
            a = jnp.concatenate([t[:BUCKET] for t in tiles] + blank, axis=0).astype(BF16)
            b = jnp.concatenate([t[BUCKET:] for t in tiles] + blank, axis=0).astype(BF16)
            span = slice(h * LANES, (h + 1) * LANES)
            a_ref[:, span] = dot(sel, a).astype(BF16)
            b_ref[:, span] = dot(sel, b).astype(BF16)

    for c in range(2):
        off = BODY_ROWS + c * 2 * BUCKET
        total = jnp.sum(in_ref[:, 0, off : off + 2 * BUCKET, :].astype(F32), axis=0)
        for half in range(2):
            span = slice((2 * c + half) * LANES, (2 * c + half + 1) * LANES)
            piece = total[half * BUCKET : (half + 1) * BUCKET]

            @pl.when(x == 0)
            def _():
                tg_ref[:, span] = piece

            @pl.when(x > 0)
            def _():
                tg_ref[:, span] += piece


def unpack(msg, dest, got):
    full = lambda shape: pl.BlockSpec(shape, lambda x: (0,) * len(shape))
    cols = pl.BlockSpec((ROWS, COLS), lambda x: (0, x))
    rows = jax.ShapeDtypeStruct((ROWS, NX * COLS), BF16)
    return pl.pallas_call(
        unpack_kernel,
        grid=(NX,),
        in_specs=[
            full((PEERS * 8, LANES)),
            full((1, LANES)),
            pl.BlockSpec((NZ, 1, MSG_ROWS, LANES), lambda x: (0, x, 0, 0)),
        ],
        out_specs=[cols, cols, cols, cols, full((BUCKET, TEXT))],
        out_shape=[rows, rows, rows, rows, jax.ShapeDtypeStruct((BUCKET, TEXT), F32)],
        scratch_shapes=[pltpu.VMEM((ROWS, COMPACT * BUCKET), BF16)],
        compiler_params=pltpu.CompilerParams(vmem_limit_bytes=24 << 20),
        name="unpack",
    )(msg, dest, got)


def exchange(x):
    return lax.all_to_all(x, "seq", split_axis=0, concat_axis=0, tiled=True)


def swap(x, axis, bit):
    size = lax.axis_size(axis)
    return lax.ppermute(x, axis, [(j, j ^ bit) for j in range(size)])


def gather_bits(x, axis, bits):
    index = lax.axis_index(axis)
    for depth, bit in enumerate(bits):
        other = swap(x, axis, bit)
        up = (index & bit) != 0
        first = jnp.where(up, other, x)
        second = jnp.where(up, x, other)
        x = jnp.stack([first, second], axis=depth)
    return x


def halve(x, axis, bit, dim, kind):
    up = (lax.axis_index(axis) & bit) != 0
    zero, one = lax.index_in_dim(x, 0, dim, False), lax.index_in_dim(x, 1, dim, False)
    return jnp.where(up, one, zero), swap(jnp.where(up, zero, one).astype(kind), axis, bit)


def x_split_kernel(x_ref, keep_ref, got_ref, *refs):
    total_ref = refs[NX]
    total_ref[...] = keep_ref[...] + got_ref[...].astype(F32)
    for f, out_ref in enumerate(refs[:NX]):
        for j in range(NZ):
            out_ref[pl.ds(j, 1), :] = total_ref[pl.ds(j * NX + (x_ref[0] ^ f), 1), :]


def join_kernel(x_ref, *refs):
    out_ref = refs[NX]
    for z in range(NZ):
        for f in range(NX):
            out_ref[z, pl.ds(f, 1), :] = refs[f][pl.ds(z, 1), :]


def row_sum_kernel(x_ref, in_ref, out_ref, total_ref):
    total = in_ref[0]
    for z in range(1, NZ):
        total = total + in_ref[z]
    total_ref[...] = total
    for c in range(NX):
        out_ref[:, c * COLS : (c + 1) * COLS] = total_ref[pl.ds(x_ref[0] ^ c, 1), :]


def small_call(kernel, outs, scratch, index, *args):
    return pl.pallas_call(
        kernel,
        out_shape=[jax.ShapeDtypeStruct(shape, kind) for shape, kind in outs],
        in_specs=[pl.BlockSpec(memory_space=pltpu.SMEM)]
        + [pl.BlockSpec(memory_space=pltpu.VMEM)] * len(args),
        scratch_shapes=scratch,
        compiler_params=pltpu.CompilerParams(vmem_limit_bytes=8 << 20),
    )(index, *args)


def reduce_weight(wg, xi):
    wg = wg.reshape(2, 2, 2, 2, PEERS, COLS)
    keep, got = halve(wg, "dp", 1, 3, BF16)
    for bit, dim in ((2, 2), (4, 1), (8, 0)):
        keep, got = halve(keep + got.astype(F32), "dp", bit, dim, BF16)
    piece = ((NZ, COLS), F32)
    parts = small_call(x_split_kernel, [piece] * NX, [pltpu.VMEM((PEERS, COLS), F32)], xi, keep, got)
    parts = [parts[0]] + [swap(parts[f], "seq", f) for f in range(1, NX)]
    lines = small_call(join_kernel, [((NZ, NX, COLS), F32)], [], xi, *parts)[0]
    groups = [[z * NX + x for z in range(NZ)] for x in range(NX)]
    lines = lax.all_to_all(lines, "seq", 0, 0, axis_index_groups=groups, tiled=True)
    row = [((1, NX * COLS), F32)]
    return small_call(row_sum_kernel, row, [pltpu.VMEM((NX, COLS), F32)], xi, lines)[0]


def local(query, key, value, text, cond_weight, cotangent, dest, segment, align):
    seq = lax.axis_index("seq").astype(jnp.int32)
    zi = (seq >> 2).reshape(1)
    xi = (seq & 3).reshape(1)
    dest_row = dest.reshape(1, ROWS)
    first = prep(dest_row, align.reshape(1, ROWS), segment.reshape(1, SLOTS), cond_weight)
    msg3 = exchange(first.reshape(PEERS, 8, LANES))
    msg = msg3.reshape(PEERS * 8, LANES)
    packed, own = pack(msg, dest_row, text, query, key, value, cotangent)
    got = exchange(packed.reshape(PEERS, MSG_ROWS, LANES))
    bias, pick = setup(zi, msg, own)
    my_w = msg3[:, 4 : 4 + HPD, :].astype(BF16).reshape(PEERS, COLS)
    full_w = gather_bits(my_w, "dp", (8, 4, 2, 1)).reshape(TEXT, COLS)
    back, wg = attend(zi, bias, pick, got, full_w)
    returned = exchange(back)
    weight_grad = reduce_weight(wg, xi)
    attended, query_grad, key_grad, value_grad, text_grad = unpack(
        msg, dest_row, returned.reshape(NZ, NX, MSG_ROWS, LANES)
    )
    return attended, query_grad, key_grad, value_grad, text_grad, weight_grad


def solution(mesh):
    rows = P(("dp", "seq"), None)
    flat = P(("dp", "seq"))
    return jax.shard_map(
        local,
        mesh=mesh,
        in_specs=(rows, rows, rows, rows, rows, rows, flat, flat, flat),
        out_specs=(rows,) * 6,
        check_vma=False,
    )
```

```python
import jax
import jax.numpy as jnp
from jax import lax
from jax.experimental import pallas as pl
from jax.experimental.pallas import tpu as pltpu
from jax.sharding import PartitionSpec as P

F32 = jnp.float32
BF16 = jnp.bfloat16

NZ, NX = 8, 4
PEERS = NZ * NX
ROWS = 128
SLOTS = 256
BUCKET = 8
OWNERS = 21
HPD = 3
UNITS = 8
COMPACT = 24
NEAR = 4
LANES = 128
COLS = HPD * LANES
TEXT = 512
GTEXT = 256
BLOCK = 2 * 2 * BUCKET
TEXT_ROWS = 32
TGR = NZ * BUCKET
BODY_ROWS = UNITS * BLOCK
MSG_ROWS = BODY_ROWS + TEXT_ROWS
STEP = 4


def iota(shape, dim):
    return lax.broadcasted_iota(jnp.int32, shape, dim)


def dot(a, b):
    return jnp.dot(a, b, preferred_element_type=F32)


def dot_nt(a, b):
    return lax.dot_general(a, b, (((1,), (1,)), ((), ())), preferred_element_type=F32)


def dot_tn(a, b):
    return lax.dot_general(a, b, (((0,), (0,)), ((), ())), preferred_element_type=F32)


def upper(n):
    return (iota((n, n), 0) <= iota((n, n), 1)).astype(BF16)


def spread8(x):
    n = x.shape[0]
    return jnp.broadcast_to(x[:, None, :], (n, BUCKET, LANES)).reshape(n * BUCKET, LANES)


def bucket_select(match):
    n = match.shape[0]
    count = dot(match.astype(BF16), upper(ROWS))
    rank = ((iota((n * BUCKET, LANES), 0) & (BUCKET - 1)) + 1).astype(F32)
    hit = (spread8(count) == rank) & (spread8(match) > 0.5)
    return jnp.where(hit, 1.0, 0.0)


def compact_owners(seg_first):
    flag = jnp.where(jnp.broadcast_to(seg_first[:, 0:1], (PEERS, LANES)) >= 0.0, 1.0, 0.0)
    lower = (iota((PEERS, PEERS), 0) >= iota((PEERS, PEERS), 1)).astype(BF16)
    count = dot(lower, flag.astype(BF16))
    lane = (iota((PEERS, LANES), 1) + 1).astype(F32)
    hit = jnp.where((count == lane) & (flag > 0.5), 1.0, 0.0)
    ids = iota((PEERS, LANES), 0).astype(F32) + 1.0
    row = jnp.sum(hit * ids, axis=0, keepdims=True) - 1.0
    diag = iota((COMPACT, LANES), 0) == iota((COMPACT, LANES), 1)
    col = jnp.sum(jnp.where(diag, jnp.broadcast_to(row, (COMPACT, LANES)), 0.0), axis=1, keepdims=True)
    return jnp.broadcast_to(col, (COMPACT, LANES))


def prep_kernel(dest_ref, align_ref, seg_ref, w_ref, out_ref):
    sub = iota((8, LANES), 0)

    def row(v):
        return jnp.broadcast_to(v.astype(F32), (8, LANES))

    base = jnp.where(sub == 0, row(dest_ref[...]), 0.0)
    base = jnp.where(sub == 1, row(align_ref[...]), base)
    seg = seg_ref[...]
    base = jnp.where(sub == 2, row(seg[:, :LANES]), base)
    base = jnp.where(sub == 3, row(seg[:, LANES:]), base)
    w = w_ref[...].astype(F32)
    for x in range(NX):
        msg = base
        for h in range(HPD):
            start = (x * HPD + h) * LANES
            msg = jnp.where(sub == 4 + h, row(w[:, start : start + LANES]), msg)
        for z in range(NZ):
            out_ref[z, x] = msg


def prep(dest, align, seg, w):
    return pl.pallas_call(
        prep_kernel,
        out_shape=jax.ShapeDtypeStruct((NZ, NX, 8, LANES), F32),
        name="prep",
    )(dest, align, seg, w)


def owner_match(msg_ref, dest_ref):
    owners = compact_owners(msg_ref[pl.ds(2, PEERS, stride=8), :])
    mine = jnp.broadcast_to(dest_ref[...] >> 8, (COMPACT, LANES)).astype(F32)
    return owners, jnp.where(mine == owners, 1.0, 0.0)


def pack_kernel(msg_ref, dest_ref, text_ref, q_ref, k_ref, v_ref, g_ref, out_ref, own_ref, sel_ref):
    @pl.when(pl.program_id(0) == 0)
    def _():
        owners, match = owner_match(msg_ref, dest_ref)
        own_ref[...] = owners
        sel_ref[...] = bucket_select(match).astype(BF16)

    sel = sel_ref[...]
    for pair, (a_ref, b_ref) in enumerate(((q_ref, k_ref), (v_ref, g_ref))):
        a = dot(sel, a_ref[...]).reshape(COMPACT, BUCKET, COLS)
        b = dot(sel, b_ref[...]).reshape(COMPACT, BUCKET, COLS)
        both = jnp.concatenate([a, b], axis=1).astype(BF16)
        for unit in range(NZ * UNITS):
            owner, h = divmod(unit, HPD)
            off = unit % UNITS * BLOCK + pair * 2 * BUCKET
            out_ref[unit // UNITS, 0, off : off + 2 * BUCKET, :] = both[owner, :, h * LANES : (h + 1) * LANES]
    text = text_ref[...].astype(F32)
    for c in range(2):
        tile = jnp.concatenate(
            [text[:, 2 * c * LANES : (2 * c + 1) * LANES], text[:, (2 * c + 1) * LANES : (2 * c + 2) * LANES]], axis=0
        ).astype(BF16)
        off = BODY_ROWS + c * 2 * BUCKET
        for z in range(NZ):
            out_ref[z, 0, off : off + 2 * BUCKET, :] = tile


def pack(msg, dest, text, q, k, v, g):
    full = lambda shape: pl.BlockSpec(shape, lambda x: (0,) * len(shape))
    cols = pl.BlockSpec((ROWS, COLS), lambda x: (0, x))
    return pl.pallas_call(
        pack_kernel,
        grid=(NX,),
        in_specs=[full((PEERS * 8, LANES)), full((1, LANES)), full((BUCKET, TEXT)), cols, cols, cols, cols],
        out_specs=[
            pl.BlockSpec((NZ, 1, MSG_ROWS, LANES), lambda x: (0, x, 0, 0)),
            full((COMPACT, LANES)),
        ],
        out_shape=[
            jax.ShapeDtypeStruct((NZ, NX, MSG_ROWS, LANES), BF16),
            jax.ShapeDtypeStruct((COMPACT, LANES), F32),
        ],
        scratch_shapes=[pltpu.VMEM((COMPACT * BUCKET, LANES), BF16)],
        name="pack",
    )(msg, dest, text, q, k, v, g)


def owner_setup(owner, msg_ref):
    n = SLOTS
    dest = msg_ref[pl.ds(0, PEERS, stride=8), :].astype(jnp.int32)
    match = jnp.where((dest >> 8).astype(F32) == owner, 1.0, 0.0)
    sel = bucket_select(match)
    valid = jnp.sum(sel, axis=1, keepdims=True)
    slot = jnp.sum(sel * spread8((dest & (SLOTS - 1)).astype(F32)), axis=1, keepdims=True)
    slot = jnp.where(valid > 0.5, slot, -1.0)
    align = jnp.sum(sel * spread8(msg_ref[pl.ds(1, PEERS, stride=8), :]), axis=1, keepdims=True)
    align = jnp.where(valid > 0.5, align, -1.0)

    mine = iota((PEERS, LANES), 0).astype(F32) == owner
    seg_lo = jnp.sum(jnp.where(mine, msg_ref[pl.ds(2, PEERS, stride=8), :], 0.0), axis=0, keepdims=True)
    seg_hi = jnp.sum(jnp.where(mine, msg_ref[pl.ds(3, PEERS, stride=8), :], 0.0), axis=0, keepdims=True)
    seg = jnp.concatenate([seg_lo, seg_hi], axis=1)
    lane = iota((n, n), 1)
    lanef = lane.astype(F32)
    diag = iota((n, n), 0) == lane
    label = jnp.sum(jnp.where(lanef == slot, jnp.broadcast_to(seg, (n, n)), 0.0), axis=1, keepdims=True)
    label = jnp.where(valid > 0.5, label, -1.0)
    label_b = jnp.broadcast_to(label, (n, n))
    label_row = jnp.sum(jnp.where(diag, label_b, 0.0), axis=0, keepdims=True)
    allowed = ((label_b == jnp.broadcast_to(label_row, (n, n))) & (label_b >= 0.0)) | diag
    pick = jnp.where(lanef == align, 1.0, 0.0).astype(BF16)
    return jnp.where(allowed, 0.0, -1e30), pick


def setup_kernel(z_ref, msg_ref, own_ref, bias_ref, pick_ref):
    owner0 = z_ref[0] * UNITS // HPD
    for t in range(NEAR):
        owner = jnp.broadcast_to(own_ref[pl.ds(owner0 + t, 1), :], (PEERS, LANES))
        bias_ref[t], pick_ref[t] = owner_setup(owner, msg_ref)


def setup(zi, msg, own):
    return pl.pallas_call(
        setup_kernel,
        in_specs=[pl.BlockSpec(memory_space=pltpu.SMEM)] + [pl.BlockSpec(memory_space=pltpu.VMEM)] * 2,
        out_shape=[
            pltpu.HBM((NEAR, SLOTS, SLOTS), F32),
            pltpu.HBM((NEAR, SLOTS, GTEXT), BF16),
        ],
        compiler_params=pltpu.CompilerParams(vmem_limit_bytes=24 << 20),
        name="setup",
    )(zi, msg, own)


def attend_kernel(
    z_ref, mask_ref, pick_ref, in_ref, tail_ref, w_ref, out_ref, wg_ref, tg_ref,
    acc_ref, text_ref, w3_ref, cond_ref, bias_ref, bias_sem,
):
    i = pl.program_id(0)
    n = SLOTS
    unit0 = z_ref[0] * UNITS
    owner0 = unit0 // HPD

    @pl.when(i == 0)
    def _():
        copy = pltpu.make_async_copy(mask_ref, bias_ref, bias_sem)
        copy.start()
        for c in range(2):
            tiles = tail_ref[:, c * 2 * BUCKET : (c + 1) * 2 * BUCKET, :].astype(F32)
            tiles = tiles.reshape(PEERS, 2, BUCKET, LANES)
            for half in range(2):
                span = slice((2 * c + half) * LANES, (2 * c + half + 1) * LANES)
                text_ref[:, span] = tiles[:, half].reshape(GTEXT, LANES).astype(BF16)
        text = text_ref[...]
        for t in range(NEAR):
            cond_ref[t] = dot(pick_ref[t], text).astype(BF16)
        for h in range(HPD):
            w3_ref[h] = w_ref[:, h * LANES : (h + 1) * LANES]
        acc_ref[...] = jnp.zeros_like(acc_ref)
        copy.wait()

    scale = LANES ** (-0.5)

    @pl.when(i < UNITS // STEP)
    def _():
        units = range(STEP)
        heads, owners = [], []
        for u in units:
            unit = unit0 + i * STEP + u
            owner = unit // HPD
            heads.append(unit - owner * HPD)
            owners.append(owner - owner0)

        def pair_of(u, pair):
            off = u * BLOCK + pair * 2 * BUCKET
            both = in_ref[:, off : off + 2 * BUCKET, :].astype(F32).reshape(PEERS, 2, BUCKET, LANES)
            return both[:, 0].reshape(n, LANES), both[:, 1].reshape(n, LANES)

        def put(u, pair, a, b):
            off = u * BLOCK + pair * 2 * BUCKET
            out_ref[:, off : off + 2 * BUCKET, :] = jnp.concatenate(
                [a.reshape(PEERS, BUCKET, LANES), b.reshape(PEERS, BUCKET, LANES)], axis=1
            ).astype(BF16)

        qk = [[x.astype(BF16) for x in pair_of(u, 0)] for u in units]
        scores = [dot_nt(q, k) for q, k in qk]
        vg = []
        for u in units:
            v, g = pair_of(u, 1)
            extra = dot(cond_ref[owners[u]], w3_ref[heads[u]])
            vg.append(((v + extra).astype(BF16), g.astype(BF16)))
        prob_grads = [dot_nt(g, v) for v, g in vg]
        probs = []
        for u in units:
            s = scores[u] * scale + bias_ref[owners[u]]
            e = jnp.exp(s - jnp.max(s, axis=1, keepdims=True))
            probs.append(e * (1.0 / jnp.sum(e, axis=1, keepdims=True)))
        weights = [p.astype(BF16) for p in probs]
        score_grads = []
        for p, pg in zip(probs, prob_grads):
            centre = jnp.sum(p * pg, axis=1, keepdims=True)
            score_grads.append((p * (pg - centre)).astype(BF16))
        for u in units:
            (q, k), (v, g) = qk[u], vg[u]
            out = dot(weights[u], v)
            value_grad = dot_tn(weights[u], g)
            query_grad = dot(score_grads[u], k) * scale
            key_grad = dot_tn(score_grads[u], q) * scale
            put(u, 0, out, query_grad)
            put(u, 1, key_grad, value_grad)
            acc_ref[heads[u]] += dot_tn(pick_ref[owners[u]], value_grad.astype(BF16))

    @pl.when(i == UNITS // STEP)
    def _():
        text = text_ref[...]
        tg = jnp.zeros((GTEXT, TEXT), F32)
        for h in range(HPD):
            acc = acc_ref[h].astype(BF16)
            tg = tg + dot_nt(acc, w3_ref[h])
            wg_ref[:, h * LANES : (h + 1) * LANES] = dot_tn(text, acc)
        tg = tg.reshape(NZ, NX, BUCKET, TEXT)
        for x in range(NX):
            tg_ref[x] = tg[:, x].reshape(NZ * BUCKET, TEXT).astype(BF16)


def attend(zi, bias, pick, got, w):
    full = lambda shape: pl.BlockSpec(shape, lambda i, z: (0,) * len(shape))
    last = UNITS // STEP - 1
    return pl.pallas_call(
        attend_kernel,
        grid_spec=pltpu.PrefetchScalarGridSpec(
            num_scalar_prefetch=1,
            grid=(UNITS // STEP + 1,),
            in_specs=[
                pl.BlockSpec(memory_space=pltpu.HBM),
                full((NEAR, SLOTS, GTEXT)),
                pl.BlockSpec((PEERS, STEP * BLOCK, LANES), lambda i, z: (0, jnp.minimum(i, last), 0)),
                pl.BlockSpec((PEERS, TEXT_ROWS, LANES), lambda i, z: (0, BODY_ROWS // TEXT_ROWS, 0)),
                full((TEXT, COLS)),
            ],
            out_specs=[
                pl.BlockSpec((PEERS, STEP * BLOCK, LANES), lambda i, z: (0, jnp.minimum(i, last), 0)),
                full((TEXT, COLS)),
                full((NX, NZ * BUCKET, TEXT)),
            ],
            scratch_shapes=[
                pltpu.VMEM((HPD, GTEXT, LANES), F32),
                pltpu.VMEM((GTEXT, TEXT), BF16),
                pltpu.VMEM((HPD, TEXT, LANES), BF16),
                pltpu.VMEM((NEAR, SLOTS, TEXT), BF16),
                pltpu.VMEM((NEAR, SLOTS, SLOTS), F32),
                pltpu.SemaphoreType.DMA,
            ],
        ),
        out_shape=[
            pltpu.HBM((PEERS, BODY_ROWS, LANES), BF16),
            pltpu.HBM((TEXT, COLS), F32),
            pltpu.HBM((NX, NZ * BUCKET, TEXT), BF16),
        ],
        compiler_params=pltpu.CompilerParams(vmem_limit_bytes=28 << 20),
        name="attend",
    )(zi, pltpu.with_memory_space_constraint(bias, pltpu.HBM), pick, got, got, w)


def unpack_kernel(msg_ref, dest_ref, in_ref, o_ref, q_ref, k_ref, v_ref, sel_ref):
    x = pl.program_id(0)

    @pl.when(x == 0)
    def _():
        _, match = owner_match(msg_ref, dest_ref)
        sel_ref[...] = jnp.transpose(bucket_select(match)).astype(BF16)

    sel = sel_ref[...]
    for pair, (a_ref, b_ref) in enumerate(((o_ref, q_ref), (k_ref, v_ref))):
        for h in range(HPD):
            tiles = []
            for owner in range(OWNERS):
                unit = owner * HPD + h
                off = unit % UNITS * BLOCK + pair * 2 * BUCKET
                tiles.append(in_ref[unit // UNITS, 0, off : off + 2 * BUCKET, :].astype(F32))
            blank = [jnp.zeros((BUCKET, LANES), F32)] * (COMPACT - OWNERS)
            a = jnp.concatenate([t[:BUCKET] for t in tiles] + blank, axis=0).astype(BF16)
            b = jnp.concatenate([t[BUCKET:] for t in tiles] + blank, axis=0).astype(BF16)
            span = slice(h * LANES, (h + 1) * LANES)
            a_ref[:, span] = dot(sel, a).astype(BF16)
            b_ref[:, span] = dot(sel, b).astype(BF16)


def unpack(msg, dest, got):
    full = lambda shape: pl.BlockSpec(shape, lambda x: (0,) * len(shape))
    cols = pl.BlockSpec((ROWS, COLS), lambda x: (0, x))
    rows = jax.ShapeDtypeStruct((ROWS, NX * COLS), BF16)
    return pl.pallas_call(
        unpack_kernel,
        grid=(NX,),
        in_specs=[
            full((PEERS * 8, LANES)),
            full((1, LANES)),
            pl.BlockSpec((NZ, 1, BODY_ROWS, LANES), lambda x: (0, x, 0, 0)),
        ],
        out_specs=[cols, cols, cols, cols],
        out_shape=[rows, rows, rows, rows],
        scratch_shapes=[pltpu.VMEM((ROWS, COMPACT * BUCKET), BF16)],
        compiler_params=pltpu.CompilerParams(vmem_limit_bytes=24 << 20),
        name="unpack",
    )(msg, dest, got)


def exchange(x):
    return lax.all_to_all(x, "seq", split_axis=0, concat_axis=0, tiled=True)


def swap(x, axis, bit):
    size = lax.axis_size(axis)
    return lax.ppermute(x, axis, [(j, j ^ bit) for j in range(size)])


def gather_bits(x, axis, bits):
    index = lax.axis_index(axis)
    for depth, bit in enumerate(bits):
        other = swap(x, axis, bit)
        up = (index & bit) != 0
        first = jnp.where(up, other, x)
        second = jnp.where(up, x, other)
        x = jnp.stack([first, second], axis=depth)
    return x


def halve(x, axis, bit, dim, kind):
    up = (lax.axis_index(axis) & bit) != 0
    zero, one = lax.index_in_dim(x, 0, dim, False), lax.index_in_dim(x, 1, dim, False)
    return jnp.where(up, one, zero), swap(jnp.where(up, zero, one).astype(kind), axis, bit)


def x_split_kernel(x_ref, keep_ref, got_ref, tg_ref, own_ref, mine_ref, *refs):
    total_ref, piece_ref = refs[NX - 1 :]
    total_ref[...] = keep_ref[...] + got_ref[...].astype(F32)
    for f in range(NX):
        target = piece_ref if f else own_ref
        for j in range(NZ):
            target[pl.ds(j, 1), :] = total_ref[pl.ds(j * NX + (x_ref[0] ^ f), 1), :]
        if f == 0:
            mine_ref[...] = tg_ref[x_ref[0]]
        else:
            send_ref = refs[f - 1]
            send_ref[:TGR, :] = tg_ref[x_ref[0] ^ f]
            rows = jnp.concatenate([piece_ref[...], jnp.zeros((NZ, COLS), F32)], axis=0)
            send_ref[TGR:, :COLS] = rows.astype(BF16)
            send_ref[TGR:, COLS:] = jnp.zeros((2 * NZ, TEXT - COLS), BF16)


def join_kernel(x_ref, own_ref, mine_ref, *refs):
    got_refs, (out_ref, weight_ref, row_ref) = refs[: NX - 1], refs[NX - 1 :]
    total = mine_ref[...].astype(F32)
    weight_ref[0] = own_ref[...]
    for f, got_ref in enumerate(got_refs, 1):
        total = total + got_ref[:TGR, :].astype(F32)
        weight_ref[f] = got_ref[TGR:, :COLS].astype(F32)[:NZ]
    total = total.reshape(NZ, BUCKET, TEXT)
    row_ref[...] = jnp.zeros_like(row_ref)
    for z in range(NZ):
        for f in range(NX):
            row_ref[z, f : f + 1, :COLS] = weight_ref[f, z : z + 1, :]
        out_ref[z] = jnp.concatenate([total[z], row_ref[z]], axis=0).astype(BF16)


def row_sum_kernel(x_ref, in_ref, out_ref, tg_ref, total_ref):
    total = in_ref[0].astype(F32)
    for z in range(1, NZ):
        total = total + in_ref[z].astype(F32)
    tg_ref[...] = total[:BUCKET]
    total_ref[...] = total[BUCKET:]
    for c in range(NX):
        out_ref[:, c * COLS : (c + 1) * COLS] = total_ref[pl.ds(x_ref[0] ^ c, 1), :COLS]


def small_call(kernel, outs, scratch, index, *args):
    return pl.pallas_call(
        kernel,
        out_shape=[jax.ShapeDtypeStruct(shape, kind) for shape, kind in outs],
        in_specs=[pl.BlockSpec(memory_space=pltpu.SMEM)]
        + [pl.BlockSpec(memory_space=pltpu.VMEM)] * len(args),
        scratch_shapes=scratch,
        compiler_params=pltpu.CompilerParams(vmem_limit_bytes=8 << 20),
    )(index, *args)


def reduce_text(wg, tg, xi):
    wg = wg.reshape(2, 2, 2, 2, PEERS, COLS)
    keep, got = halve(wg, "dp", 1, 3, BF16)
    for bit, dim in ((2, 2), (4, 1), (8, 0)):
        keep, got = halve(keep + got.astype(F32), "dp", bit, dim, BF16)
    outs = [((NZ, COLS), F32), ((TGR, TEXT), BF16)] + [((TGR + 2 * NZ, TEXT), BF16)] * (NX - 1)
    scratch = [pltpu.VMEM((PEERS, COLS), F32), pltpu.VMEM((NZ, COLS), F32)]
    own, mine, *sends = small_call(x_split_kernel, outs, scratch, xi, keep, got, tg)
    parts = [own, mine] + [swap(send, "seq", f) for f, send in enumerate(sends, 1)]
    scratch = [pltpu.VMEM((NX, NZ, COLS), F32), pltpu.VMEM((NZ, BUCKET, TEXT), F32)]
    lines = small_call(join_kernel, [((NZ, 2 * BUCKET, TEXT), BF16)], scratch, xi, *parts)[0]
    groups = [[z * NX + x for z in range(NZ)] for x in range(NX)]
    lines = lax.all_to_all(lines, "seq", 0, 0, axis_index_groups=groups, tiled=True)
    outs = [((1, NX * COLS), F32), ((BUCKET, TEXT), F32)]
    return small_call(row_sum_kernel, outs, [pltpu.VMEM((BUCKET, TEXT), F32)], xi, lines)


def local(query, key, value, text, cond_weight, cotangent, dest, segment, align):
    seq = lax.axis_index("seq").astype(jnp.int32)
    zi = (seq >> 2).reshape(1)
    xi = (seq & 3).reshape(1)
    dest_row = dest.reshape(1, ROWS)
    first = prep(dest_row, align.reshape(1, ROWS), segment.reshape(1, SLOTS), cond_weight)
    msg3 = exchange(first.reshape(PEERS, 8, LANES))
    msg = msg3.reshape(PEERS * 8, LANES)
    packed, own = pack(msg, dest_row, text, query, key, value, cotangent)
    got = exchange(packed.reshape(PEERS, MSG_ROWS, LANES))
    bias, pick = setup(zi, msg, own)
    my_w = msg3[:, 4 : 4 + HPD, :].astype(BF16).reshape(PEERS, COLS)
    full_w = gather_bits(my_w, "dp", (8, 4, 2, 1)).reshape(TEXT, COLS)
    back, wg, tg = attend(zi, bias, pick, got, full_w)
    returned = exchange(back)
    weight_grad, text_grad = reduce_text(wg, tg, xi)
    attended, query_grad, key_grad, value_grad = unpack(
        msg, dest_row, returned.reshape(NZ, NX, BODY_ROWS, LANES)
    )
    return attended, query_grad, key_grad, value_grad, text_grad, weight_grad


def solution(mesh):
    rows = P(("dp", "seq"), None)
    flat = P(("dp", "seq"))
    return jax.shard_map(
        local,
        mesh=mesh,
        in_specs=(rows, rows, rows, rows, rows, rows, flat, flat, flat),
        out_specs=(rows,) * 6,
        check_vma=False,
    )
```
